32 devices in a mesh: date: 2 (over y), trade: 8 (over z, x), path: 2 (over core).
Axes of the slice: x: 2, y: 2, z: 4, core: 2. Of those that a mesh axis runs over, the one named last changes fastest.
Arguments:
- basis_values: bfloat16 [2048, 512], P(('date', 'path')), parts along dimension 0, may hold values from -6 to 6
- coefficients: bfloat16 [2560, 512], P(('date', 'trade')), parts along dimension 0, may hold values from -0.25 to 0.25
- trade_cpty: int32 [1280], P('trade'), may hold values from 0 to 127, as said below
- trade_bucket: int32 [1280], P('trade'), may hold values from 0 to 127
- risk_weights: float32 [128], replicated, may hold values from 0.5 to 2
- correlation: float32 [128, 128], replicated, may hold values from 0 to 1, as said below
- funding_spread: float32 [128], P('trade'), may hold values from 0.5 to 2
Outputs:
- margin: float32 [128, 2048], P('trade', ('date', 'path')), parts along dimension 1
- basis_adjoint: bfloat16 [2048, 512], P(('date', 'path')), parts along dimension 0
The draws below stay inside these ranges and needn't reach their ends.
There are 2 independent parts, one for each index of `date`. The reference program is written for one: setup_inputs(seed, part) draws one part's arguments, and reference() takes and returns one part's arrays. A program takes and returns all parts, laid end to end along the dimension named above; an argument that names none is the same for every part. Nothing has to cross between parts.
Inputs may be any that keep to these rules, and one draw needn't show every extreme that they name: `trade_cpty`: counterparty c belongs to owner block c // 16. Among the trades of one device, at most 40 belong to counterparties of one owner block; in every draw one owner block receives exactly 40 from every device. Counterparties differ in size. `correlation`: symmetric positive definite with unit diagonal; smallest eigenvalue at least 0.01; entries positive.
All inputs are finite; a program needn't handle non-finite values.
Results may differ from the reference program's by a relative error of at most 0.0034.
Values may be sent and summed in bfloat16 or wider, within the bound.
No kernel may reach another device: no remote copies, remote signals or barrier semaphores. Data moves between devices by JAX's collectives and lax.ppermute only.
A program may use at most 64 MiB of HBM per device.

```python
import math
import jax
import jax.numpy as jnp
from jax import lax

BASIS = 512
BUCKETS = 128
CP_DEV = 16
TRADE_DEV = 160
CAP = 40
COUNTERPARTIES = 128
TRADES = 1280
PATHS = 1024
N_TRADE = 8


def draw_trade_cpty(key, part):
    slot_total = N_TRADE * CAP
    starred = jax.random.randint(jax.random.fold_in(key, 7), (), 0, N_TRADE)
    shifts = jax.random.randint(jax.random.fold_in(key, 11), (N_TRADE,), 0, CP_DEV)

    def one_device(device_index):
        device_key = jax.random.fold_in(key, device_index + 100)
        ranks = jax.random.permutation(jax.random.fold_in(device_key, 1), slot_total).astype(jnp.int32)
        slot_owner = jnp.arange(slot_total, dtype=jnp.int32) // CAP
        scores = jnp.where(slot_owner == starred, ranks - slot_total, ranks)
        picked = jnp.argsort(scores)[:TRADE_DEV].astype(jnp.int32)
        owner_of = picked // CAP
        first_pick = jax.random.randint(jax.random.fold_in(device_key, 2), (TRADE_DEV,), 0, CP_DEV)
        second_pick = jax.random.randint(jax.random.fold_in(device_key, 3), (TRADE_DEV,), 0, CP_DEV)
        local_cpty = (jnp.minimum(first_pick, second_pick) + shifts[owner_of]) % CP_DEV
        return (owner_of * CP_DEV + local_cpty).astype(jnp.int32)
    return jax.vmap(one_device)(jnp.arange(N_TRADE, dtype=jnp.int32)).reshape(-1).astype(jnp.int32)


def draw_correlation(key, part):
    block_width = 16
    blocks_count = BUCKETS // block_width
    increments = jax.random.randint(jax.random.fold_in(key, 1), (BUCKETS,), 2, 9).astype(jnp.float32)
    tenor_points = jnp.cumsum(increments)
    loading = jax.random.uniform(jax.random.fold_in(key, 2), (blocks_count,), jnp.float32, 0.4, 0.7)
    bucket_ids = jnp.arange(BUCKETS, dtype=jnp.int32)
    currency = bucket_ids // block_width
    common = loading[currency]
    own_part = jnp.sqrt(1.0 - common * common)
    same_block = currency[:, None] == currency[None, :]
    decay_part = jnp.exp(-0.02 * jnp.abs(tenor_points[:, None] - tenor_points[None, :]))
    within = jnp.where(same_block, own_part[:, None] * own_part[None, :] * decay_part, 0.0)
    result = common[:, None] * common[None, :] + within
    diagonal_mask = bucket_ids[:, None] == bucket_ids[None, :]
    return jnp.where(diagonal_mask, 1.0, result).astype(jnp.float32)


def plant(values, rng, smallest, top_value):
    dims = values.shape
    spot = [jax.random.randint(jax.random.fold_in(rng, axis), (), 0, dims[axis]) for axis in range(len(dims))]
    values = values.at[tuple(spot)].set(smallest)
    longest = dims.index(max(dims))
    spot[longest] = (spot[longest] + 1) % dims[longest]
    return values.at[tuple(spot)].set(top_value)


def steps_of(stream_key, dims, split, low, top_value):
    level = 1.0
    for axis_at, shards_of in split:
        heights = jax.random.uniform(jax.random.fold_in(jax.random.fold_in(stream_key, 6), axis_at), (shards_of,), jnp.float32, low / len(split), top_value / len(split))
        level = level * jnp.repeat(jnp.exp(heights), dims[axis_at] // shards_of).reshape((-1,) + (1,) * (len(dims) - 1 - axis_at))
    return level


def gaussian(rng, extent, deviation, bound, cuts=(), held_as=jnp.bfloat16):
    entries = jax.random.normal(rng, extent, jnp.float32) * deviation
    if len(cuts) > 0:
        entries = steps_of(rng, extent, cuts, -0.22, 0.18) * entries
    return jnp.clip(entries, min=-bound, max=bound).astype(held_as)


def setup_inputs(seed: int = 0, part: int = 0) -> dict:
    splits = jax.random.split(jax.random.key(seed), 8)
    part_keys = jax.random.split(jax.random.fold_in(splits[7], part), 8)
    basis_values = gaussian(part_keys[0], (PATHS, BASIS), 1.0, 6.0, ((0, 2),))
    coefficients = gaussian(part_keys[1], (TRADES, BASIS), BASIS ** -0.5, 0.25, ((0, 8),))
    trade_cpty = draw_trade_cpty(jax.random.fold_in(splits[7], 71), part)
    trade_bucket = plant(jax.random.randint(splits[3], (TRADES,), 0, BUCKETS), jax.random.fold_in(splits[3], 1), 0, BUCKETS - 1).astype(jnp.int32)
    risk_weights = jnp.clip(jnp.exp(jax.random.uniform(splits[4], (BUCKETS,), jnp.float32, math.log(0.5), math.log(2.0))), 0.5, 2.0)
    correlation = draw_correlation(jax.random.fold_in(splits[7], 71), part)
    funding_spread = jnp.clip(jnp.exp(math.log(2.0) - 1.3862944 * jax.random.uniform(splits[6], (COUNTERPARTIES,), jnp.float32) ** steps_of(splits[6], (COUNTERPARTIES,), ((0, 8),), -0.2, 0.2)), 0.5, 2.0)
    return dict(basis_values=basis_values, coefficients=coefficients, trade_cpty=trade_cpty, trade_bucket=trade_bucket, risk_weights=risk_weights, correlation=correlation, funding_spread=funding_spread)


def reference(basis_values, coefficients, trade_cpty, trade_bucket, risk_weights, correlation, funding_spread):
    block_rows = 256 if PATHS % 256 == 0 else PATHS
    blocks_count = PATHS // block_rows
    trade_code = (trade_cpty * BUCKETS + trade_bucket).astype(jnp.int32)
    path_blocks = basis_values.reshape(blocks_count, block_rows, BASIS)

    def one_block(basis_block):
        delta_rows = jnp.dot(basis_block, coefficients.T, preferred_element_type=jnp.float32).astype(jnp.bfloat16)
        sens_flat = jax.ops.segment_sum(delta_rows.T.astype(jnp.float32), trade_code, num_segments=COUNTERPARTIES * BUCKETS)
        sens = sens_flat.reshape(COUNTERPARTIES, BUCKETS, block_rows)
        weighted = sens * risk_weights[None, :, None]
        rho_w = jnp.einsum('cbp,db->cdp', weighted, correlation, precision=lax.Precision.HIGHEST)
        margin_now = jnp.sqrt(lax.optimization_barrier(jnp.sum(weighted * rho_w, axis=1)) + 1e-06)
        sens_bar = funding_spread[:, None, None] * risk_weights[None, :, None] * rho_w / margin_now[:, None, :]
        delta_bar = sens_bar.reshape(COUNTERPARTIES * BUCKETS, block_rows)[trade_code].astype(jnp.bfloat16)
        adjoint_rows = jnp.dot(delta_bar.T, coefficients, preferred_element_type=jnp.float32).astype(jnp.bfloat16)
        return (margin_now, adjoint_rows)
    margin_blocks, adjoint_blocks = lax.map(one_block, path_blocks)
    margin = jnp.transpose(margin_blocks, (1, 0, 2)).reshape(COUNTERPARTIES, PATHS)
    basis_adjoint = adjoint_blocks.reshape(PATHS, BASIS)
    return (margin, basis_adjoint)
```

```python
import jax
import jax.numpy as jnp
from jax import lax
from jax.experimental import pallas as pl
from jax.experimental.pallas import tpu as pltpu
from jax.sharding import PartitionSpec as P

F32 = jnp.float32
BF16 = jnp.bfloat16
BLOCK = 256
META_LANES = 256


def margin_terms(arrived, got_codes, risk_weights, correlation, funding_spread):
    path_rows = arrived.shape[0]
    cpty_count = funding_spread.shape[0]
    bucket_count = risk_weights.shape[0]
    is_filled = got_codes >= 0
    column_ids = jnp.arange(cpty_count * bucket_count, dtype=jnp.int32)
    hot_table = (got_codes[:, None] == column_ids[None, :]).astype(jnp.bfloat16)
    bucket_sums = jnp.dot(arrived, hot_table, preferred_element_type=jnp.float32)
    weighted = (
        bucket_sums.reshape(path_rows, cpty_count, bucket_count) * risk_weights[None, None, :]
    )
    rho_w = jnp.einsum("pcb,db->pcd", weighted, correlation, precision=lax.Precision.HIGHEST)
    margin_now = jnp.sqrt(jnp.sum(weighted * rho_w, axis=2) + 1e-06)
    sens_bar = (
        funding_spread[None, :, None] * risk_weights[None, None, :] * rho_w / margin_now[:, :, None]
    )
    flat_bar = sens_bar.reshape(path_rows, cpty_count * bucket_count)
    safe_codes = jnp.where(is_filled, got_codes, 0)
    slot_bar = jnp.take(flat_bar, safe_codes, axis=1) * is_filled[None, :].astype(jnp.float32)
    return (margin_now, slot_bar.astype(jnp.bfloat16))


def exchange_body(
    basis_values, coefficients, trade_cpty, trade_bucket, risk_weights, correlation, funding_spread
):
    owners = lax.axis_size("trade")
    per_device = coefficients.shape[0]
    capacity = max(2, 2 * per_device // owners)
    slot_total = owners * capacity
    cpty_count = funding_spread.shape[0]
    bucket_count = risk_weights.shape[0]
    path_rows = basis_values.shape[0]
    owner_of = trade_cpty // cpty_count
    trade_code = trade_cpty % cpty_count * bucket_count + trade_bucket
    position = jnp.arange(per_device, dtype=jnp.int32)
    same_owner = owner_of[:, None] == owner_of[None, :]
    earlier = position[None, :] < position[:, None]
    rank_in = jnp.sum((same_owner & earlier).astype(jnp.int32), axis=1)
    slot_index = owner_of * capacity + rank_in
    codes_out = jnp.full((slot_total,), -1, jnp.int32).at[slot_index].set(trade_code)
    got_codes = lax.all_to_all(codes_out, "trade", split_axis=0, concat_axis=0, tiled=True)
    delta_rows = lax.dot_general(
        basis_values, coefficients, (((1,), (1,)), ((), ())), preferred_element_type=jnp.float32
    ).astype(jnp.bfloat16)
    outgoing = jnp.zeros((path_rows, slot_total), jnp.bfloat16).at[:, slot_index].set(delta_rows)
    arrived = lax.all_to_all(outgoing, "trade", split_axis=1, concat_axis=1, tiled=True)
    margin_now, slot_bar = margin_terms(
        arrived, got_codes, risk_weights, correlation, funding_spread
    )
    returned = lax.all_to_all(slot_bar, "trade", split_axis=1, concat_axis=1, tiled=True)
    delta_bar = returned[:, slot_index]
    partial_adj = jnp.dot(delta_bar, coefficients, preferred_element_type=jnp.float32)
    basis_adjoint = lax.psum(partial_adj, "trade").astype(jnp.bfloat16)
    return (margin_now.T, basis_adjoint)


def dot(a, b):
    return jnp.dot(a, b, preferred_element_type=F32)


def split(x):
    hi = x.astype(BF16)
    return hi, (x - hi.astype(F32)).astype(BF16)


def one_hot_t(row, count):
    ids = lax.broadcasted_iota(jnp.int32, (count, row.shape[1]), 0).astype(F32)
    return (ids == row).astype(F32).astype(BF16)


def all_trades_kernel(place_ref, basis_ref, weight_ref, corr_ref, *refs, shards, per, cpties):
    meta_refs, coef_refs = refs[:shards], refs[shards : 2 * shards]
    margin_ref, adj_ref = refs[2 * shards : 2 * shards + 2]
    coef, meta, spread, delta, m_hi, m_lo, r_all, bar, sem = refs[2 * shards + 2 :]
    trades = shards * per
    groups = shards * cpties
    buckets = corr_ref.shape[0]
    copies = [
        pltpu.make_async_copy(coef_refs[s], coef.at[pl.ds(s * per, per)], sem.at[s])
        for s in range(shards)
    ]
    for copy in copies:
        copy.start()
    for s in range(shards):
        meta[:, s * per : (s + 1) * per] = meta_refs[s][:, :per]
        spread[:, s * cpties : (s + 1) * cpties] = meta_refs[s][3:4, :cpties]
    me, core = place_ref[0], place_ref[1]
    slot = meta[0:1, :].astype(jnp.int32) ^ me
    slot = jnp.where(slot >= 2, slot ^ core, slot)
    group = (slot * cpties).astype(F32) + meta[1:2, :]
    bucket = meta[2:3, :]
    group_t = one_hot_t(group, groups)
    group_hot = group_t.T
    bucket_t = one_hot_t(bucket, buckets)
    bucket_hot = bucket_t.T
    weight = weight_ref[...]
    weight_col = jnp.broadcast_to(weight, (buckets, buckets)).T
    c_hi, c_lo = split(corr_ref[...] * weight * weight_col)
    gathered = jnp.concatenate(
        [dot(c_hi, bucket_t).astype(BF16), dot(c_lo, bucket_t).astype(BF16)], 0
    )
    bucket_two = jnp.concatenate([bucket_hot, bucket_hot], 1)
    group_col = jnp.broadcast_to(group, (groups, trades)).T[:, :1]
    blocks = [slice(k, min(k + BLOCK, trades)) for k in range(0, trades, BLOCK)]
    for cols in blocks:
        for rows in blocks:
            pair = dot(bucket_two[rows], gathered[:, cols])
            pair = jnp.where(group_col[rows] == group[:, cols], pair, 0.0)
            hi, lo = split(pair)
            m_hi[rows, cols] = hi
            m_lo[rows, cols] = lo
    for copy in copies:
        copy.wait()
    for cols in blocks:
        delta[:, cols] = lax.dot_general(
            basis_ref[...], coef[cols, :], (((1,), (1,)), ((), ())), preferred_element_type=F32
        ).astype(BF16)
    squares = None
    for cols in blocks:
        r = dot(delta[...], m_hi[:, cols]) + dot(delta[...], m_lo[:, cols])
        r_all[:, cols] = r
        hi, lo = split(delta[:, cols].astype(F32) * r)
        part = dot(hi, group_hot[cols]) + dot(lo, group_hot[cols])
        squares = part if squares is None else squares + part
    margin = jnp.sqrt(squares + 1e-06)
    margin_ref[...] = margin.T[:cpties]
    hi, lo = split(spread[...] / margin)
    scale = jnp.concatenate([hi, lo], 1)
    group_two = jnp.concatenate([group_t, group_t], 0)
    for cols in blocks:
        bar[:, cols] = (r_all[:, cols] * dot(scale, group_two[:, cols])).astype(BF16)
    adj_ref[...] = dot(bar[...], coef[...]).astype(BF16)


def swap_cores(x):
    return lax.ppermute(x, "path", [(0, 1), (1, 0)])


def fetch(x, first, second, owners):
    pairs = [(i * 2, (i ^ first) * 2) for i in range(owners)]
    pairs += [(i * 2 + 1, (i ^ second) * 2 + 1) for i in range(owners)]
    return lax.ppermute(x, ("trade", "path"), pairs)


def gather_shards(x, owners):
    far = fetch(x, 4, 5, owners)
    farther = fetch(x, 6, 7, owners)
    near = fetch(x, 2, 3, owners)
    beside = fetch(x, 1, 1, owners)
    return [x, beside, near, swap_cores(near), far, swap_cores(far), farther, swap_cores(farther)]


def gather_body(
    basis_values, coefficients, trade_cpty, trade_bucket, risk_weights, correlation, funding_spread
):
    owners = lax.axis_size("trade")
    per = coefficients.shape[0]
    cpties = funding_spread.shape[0]
    buckets = risk_weights.shape[0]
    paths, width = basis_values.shape
    trades = owners * per

    def row(x):
        return jnp.pad(x.astype(F32), (0, META_LANES - x.shape[0]))

    meta = jnp.stack(
        [
            row(trade_cpty // cpties),
            row(trade_cpty % cpties),
            row(trade_bucket),
            row(funding_spread),
        ]
    )
    meta = jnp.pad(meta, ((0, 4), (0, 0)))
    coef_all = gather_shards(coefficients, owners)
    meta_all = gather_shards(meta, owners)
    place = jnp.stack([lax.axis_index("trade"), lax.axis_index("path")]).astype(jnp.int32)
    vmem = pl.BlockSpec(memory_space=pltpu.VMEM)

    def kernel(*refs):
        all_trades_kernel(*refs, shards=owners, per=per, cpties=cpties)

    return pl.pallas_call(
        kernel,
        out_shape=[
            jax.ShapeDtypeStruct((cpties, paths), F32),
            jax.ShapeDtypeStruct((paths, width), BF16),
        ],
        in_specs=[pl.BlockSpec(memory_space=pltpu.SMEM)]
        + [vmem] * (3 + owners)
        + [pl.BlockSpec(memory_space=pl.ANY)] * owners,
        out_specs=[vmem, vmem],
        scratch_shapes=[
            pltpu.VMEM((trades, width), BF16),
            pltpu.VMEM((8, trades), F32),
            pltpu.VMEM((1, owners * cpties), F32),
            pltpu.VMEM((paths, trades), BF16),
            pltpu.VMEM((trades, trades), BF16),
            pltpu.VMEM((trades, trades), BF16),
            pltpu.VMEM((paths, trades), F32),
            pltpu.VMEM((paths, trades), BF16),
            pltpu.SemaphoreType.DMA((owners,)),
        ],
        compiler_params=pltpu.CompilerParams(vmem_limit_bytes=56 << 20),
    )(place, basis_values, risk_weights.reshape(1, buckets), correlation, *meta_all, *coef_all)


def solution(mesh):
    placed = (
        P(("date", "path"), None),
        P(("date", "trade"), None),
        P("trade"),
        P("trade"),
        P(),
        P(),
        P("trade"),
    )
    small = mesh.shape["trade"] == 8 and mesh.shape["path"] == 2
    return jax.shard_map(
        gather_body if small else exchange_body,
        mesh=mesh,
        in_specs=placed,
        out_specs=(P("trade", ("date", "path")), P(("date", "path"), None)),
        check_vma=False,
    )
```

```python
import jax
import jax.numpy as jnp
from jax import lax
from jax.experimental import pallas as pl
from jax.experimental.pallas import tpu as pltpu
from jax.sharding import PartitionSpec as P

F32 = jnp.float32
BF16 = jnp.bfloat16
BLOCK = 256
META_ROWS = 8


def margin_terms(arrived, got_codes, risk_weights, correlation, funding_spread):
    path_rows = arrived.shape[0]
    cpty_count = funding_spread.shape[0]
    bucket_count = risk_weights.shape[0]
    is_filled = got_codes >= 0
    column_ids = jnp.arange(cpty_count * bucket_count, dtype=jnp.int32)
    hot_table = (got_codes[:, None] == column_ids[None, :]).astype(jnp.bfloat16)
    bucket_sums = jnp.dot(arrived, hot_table, preferred_element_type=jnp.float32)
    weighted = (
        bucket_sums.reshape(path_rows, cpty_count, bucket_count) * risk_weights[None, None, :]
    )
    rho_w = jnp.einsum("pcb,db->pcd", weighted, correlation, precision=lax.Precision.HIGHEST)
    margin_now = jnp.sqrt(jnp.sum(weighted * rho_w, axis=2) + 1e-06)
    sens_bar = (
        funding_spread[None, :, None] * risk_weights[None, None, :] * rho_w / margin_now[:, :, None]
    )
    flat_bar = sens_bar.reshape(path_rows, cpty_count * bucket_count)
    safe_codes = jnp.where(is_filled, got_codes, 0)
    slot_bar = jnp.take(flat_bar, safe_codes, axis=1) * is_filled[None, :].astype(jnp.float32)
    return (margin_now, slot_bar.astype(jnp.bfloat16))


def exchange_body(
    basis_values, coefficients, trade_cpty, trade_bucket, risk_weights, correlation, funding_spread
):
    owners = lax.axis_size("trade")
    per_device = coefficients.shape[0]
    capacity = max(2, 2 * per_device // owners)
    slot_total = owners * capacity
    cpty_count = funding_spread.shape[0]
    bucket_count = risk_weights.shape[0]
    path_rows = basis_values.shape[0]
    owner_of = trade_cpty // cpty_count
    trade_code = trade_cpty % cpty_count * bucket_count + trade_bucket
    position = jnp.arange(per_device, dtype=jnp.int32)
    same_owner = owner_of[:, None] == owner_of[None, :]
    earlier = position[None, :] < position[:, None]
    rank_in = jnp.sum((same_owner & earlier).astype(jnp.int32), axis=1)
    slot_index = owner_of * capacity + rank_in
    codes_out = jnp.full((slot_total,), -1, jnp.int32).at[slot_index].set(trade_code)
    got_codes = lax.all_to_all(codes_out, "trade", split_axis=0, concat_axis=0, tiled=True)
    delta_rows = lax.dot_general(
        basis_values, coefficients, (((1,), (1,)), ((), ())), preferred_element_type=jnp.float32
    ).astype(jnp.bfloat16)
    outgoing = jnp.zeros((path_rows, slot_total), jnp.bfloat16).at[:, slot_index].set(delta_rows)
    arrived = lax.all_to_all(outgoing, "trade", split_axis=1, concat_axis=1, tiled=True)
    margin_now, slot_bar = margin_terms(
        arrived, got_codes, risk_weights, correlation, funding_spread
    )
    returned = lax.all_to_all(slot_bar, "trade", split_axis=1, concat_axis=1, tiled=True)
    delta_bar = returned[:, slot_index]
    partial_adj = jnp.dot(delta_bar, coefficients, preferred_element_type=jnp.float32)
    basis_adjoint = lax.psum(partial_adj, "trade").astype(jnp.bfloat16)
    return (margin_now.T, basis_adjoint)


def dot(a, b):
    return jnp.dot(a, b, preferred_element_type=F32)


def split(x):
    hi = x.astype(BF16)
    return hi, (x - hi.astype(F32)).astype(BF16)


def one_hot_t(row, count):
    ids = lax.broadcasted_iota(jnp.int32, (count, row.shape[1]), 0).astype(F32)
    return (ids == row).astype(F32).astype(BF16)


def pack_kernel(cpty_ref, bucket_ref, spread_ref, coef_ref, out_ref, meta, sem, *, cpties):
    per, width = coef_ref.shape
    body = pltpu.make_async_copy(coef_ref, out_ref.at[pl.ds(0, per)], sem.at[0])
    body.start()
    cpty = cpty_ref[...]
    owner = cpty // cpties
    meta[...] = jnp.zeros_like(meta)
    meta[0:1, :per] = owner.astype(F32)
    meta[1:2, :per] = (cpty - owner * cpties).astype(F32)
    meta[2:3, :per] = bucket_ref[...].astype(F32)
    spread = spread_ref[...]
    high = spread.astype(BF16).astype(F32)
    middle = (spread - high).astype(BF16).astype(F32)
    meta[3:4, :cpties] = high
    meta[4:5, :cpties] = middle
    meta[5:6, :cpties] = spread - high - middle
    rows = meta.shape[0]

    def tail(block):
        block[...] = meta[...].astype(BF16)
        copy = pltpu.make_async_copy(block, out_ref.at[pl.ds(per, rows)], sem.at[1])
        copy.start()
        copy.wait()

    pl.run_scoped(tail, pltpu.VMEM((rows, width), BF16))
    body.wait()


def all_trades_kernel(place_ref, basis_ref, weight_ref, corr_ref, *refs, shards, per, cpties):
    shard_refs = refs[:shards]
    margin_ref, adj_ref = refs[shards : shards + 2]
    coef, tails, meta, spread, delta, m_hi, m_lo, r_all, bar, sem = refs[shards + 2 :]
    trades = shards * per
    groups = shards * cpties
    buckets = corr_ref.shape[0]
    heads = [
        pltpu.make_async_copy(
            shard_refs[s].at[pl.ds(per, META_ROWS)], tails.at[pl.ds(s * META_ROWS, META_ROWS)], sem.at[s]
        )
        for s in range(shards)
    ]
    copies = [
        pltpu.make_async_copy(
            shard_refs[s].at[pl.ds(0, per)], coef.at[pl.ds(s * per, per)], sem.at[shards + s]
        )
        for s in range(shards)
    ]
    for copy in heads + copies:
        copy.start()
    for copy in heads:
        copy.wait()
    for s in range(shards):
        tail = tails[s * META_ROWS : (s + 1) * META_ROWS, :].astype(F32)
        meta[:, s * per : (s + 1) * per] = tail[:, :per]
        spread[:, s * cpties : (s + 1) * cpties] = (
            tail[3:4, :cpties] + tail[4:5, :cpties] + tail[5:6, :cpties]
        )
    me, core = place_ref[0], place_ref[1]
    slot = meta[0:1, :].astype(jnp.int32) ^ me
    slot = jnp.where(slot >= 2, slot ^ core, slot)
    group = (slot * cpties).astype(F32) + meta[1:2, :]
    bucket = meta[2:3, :]
    group_t = one_hot_t(group, groups)
    group_hot = group_t.T
    bucket_t = one_hot_t(bucket, buckets)
    bucket_hot = bucket_t.T
    weight = weight_ref[...]
    weight_col = jnp.broadcast_to(weight, (buckets, buckets)).T
    c_hi, c_lo = split(corr_ref[...] * weight * weight_col)
    gathered = jnp.concatenate(
        [dot(c_hi, bucket_t).astype(BF16), dot(c_lo, bucket_t).astype(BF16)], 0
    )
    bucket_two = jnp.concatenate([bucket_hot, bucket_hot], 1)
    group_col = jnp.broadcast_to(group, (groups, trades)).T[:, :1]
    blocks = [slice(k, min(k + BLOCK, trades)) for k in range(0, trades, BLOCK)]
    for cols in blocks:
        for rows in blocks:
            pair = dot(bucket_two[rows], gathered[:, cols])
            pair = jnp.where(group_col[rows] == group[:, cols], pair, 0.0)
            hi, lo = split(pair)
            m_hi[rows, cols] = hi
            m_lo[rows, cols] = lo
    for copy in copies:
        copy.wait()
    for cols in blocks:
        delta[:, cols] = lax.dot_general(
            basis_ref[...], coef[cols, :], (((1,), (1,)), ((), ())), preferred_element_type=F32
        ).astype(BF16)
    for cols in blocks:
        r_all[:, cols] = dot(delta[...], m_hi[:, cols]) + dot(delta[...], m_lo[:, cols])
    squares = None
    for cols in blocks:
        hi, lo = split(delta[:, cols].astype(F32) * r_all[:, cols])
        part = dot(hi, group_hot[cols]) + dot(lo, group_hot[cols])
        squares = part if squares is None else squares + part
    margin = jnp.sqrt(squares + 1e-06)
    margin_ref[...] = margin.T[:cpties]
    hi, lo = split(spread[...] / margin)
    scale = jnp.concatenate([hi, lo], 1)
    group_two = jnp.concatenate([group_t, group_t], 0)
    for cols in blocks:
        bar[:, cols] = (r_all[:, cols] * dot(scale, group_two[:, cols])).astype(BF16)
    adj_ref[...] = dot(bar[...], coef[...]).astype(BF16)


def swap_cores(x):
    return lax.ppermute(x, "path", [(0, 1), (1, 0)])


def fetch(x, first, second, owners):
    pairs = [(i * 2, (i ^ first) * 2) for i in range(owners)]
    pairs += [(i * 2 + 1, (i ^ second) * 2 + 1) for i in range(owners)]
    return lax.ppermute(x, ("trade", "path"), pairs)


def gather_shards(x, owners):
    far = fetch(x, 4, 5, owners)
    farther = fetch(x, 6, 7, owners)
    near = fetch(x, 2, 3, owners)
    beside = fetch(x, 1, 1, owners)
    return [x, beside, near, swap_cores(near), far, swap_cores(far), farther, swap_cores(farther)]


def gather_body(
    basis_values, coefficients, trade_cpty, trade_bucket, risk_weights, correlation, funding_spread
):
    owners = lax.axis_size("trade")
    per = coefficients.shape[0]
    cpties = funding_spread.shape[0]
    buckets = risk_weights.shape[0]
    paths, width = basis_values.shape
    trades = owners * per
    vmem = pl.BlockSpec(memory_space=pltpu.VMEM)
    anywhere = pl.BlockSpec(memory_space=pl.ANY)

    def pack(*refs):
        pack_kernel(*refs, cpties=cpties)

    payload = pl.pallas_call(
        pack,
        out_shape=jax.ShapeDtypeStruct((per + META_ROWS, width), BF16),
        in_specs=[vmem, vmem, vmem, anywhere],
        out_specs=anywhere,
        scratch_shapes=[pltpu.VMEM((META_ROWS, width), F32), pltpu.SemaphoreType.DMA((2,))],
    )(
        trade_cpty.reshape(1, per),
        trade_bucket.reshape(1, per),
        funding_spread.reshape(1, cpties),
        coefficients,
    )
    gathered = gather_shards(payload, owners)
    place = jnp.stack([lax.axis_index("trade"), lax.axis_index("path")]).astype(jnp.int32)

    def kernel(*refs):
        all_trades_kernel(*refs, shards=owners, per=per, cpties=cpties)

    return pl.pallas_call(
        kernel,
        out_shape=[
            jax.ShapeDtypeStruct((cpties, paths), F32),
            jax.ShapeDtypeStruct((paths, width), BF16),
        ],
        in_specs=[pl.BlockSpec(memory_space=pltpu.SMEM)] + [vmem] * 3 + [anywhere] * owners,
        out_specs=[vmem, vmem],
        scratch_shapes=[
            pltpu.VMEM((trades, width), BF16),
            pltpu.VMEM((owners * META_ROWS, width), BF16),
            pltpu.VMEM((META_ROWS, trades), F32),
            pltpu.VMEM((1, owners * cpties), F32),
            pltpu.VMEM((paths, trades), BF16),
            pltpu.VMEM((trades, trades), BF16),
            pltpu.VMEM((trades, trades), BF16),
            pltpu.VMEM((paths, trades), F32),
            pltpu.VMEM((paths, trades), BF16),
            pltpu.SemaphoreType.DMA((2 * owners,)),
        ],
        compiler_params=pltpu.CompilerParams(vmem_limit_bytes=40 << 20),
    )(place, basis_values, risk_weights.reshape(1, buckets), correlation, *gathered)


def solution(mesh):
    placed = (
        P(("date", "path"), None),
        P(("date", "trade"), None),
        P("trade"),
        P("trade"),
        P(),
        P(),
        P("trade"),
    )
    small = mesh.shape["trade"] == 8 and mesh.shape["path"] == 2
    return jax.shard_map(
        gather_body if small else exchange_body,
        mesh=mesh,
        in_specs=placed,
        out_specs=(P("trade", ("date", "path")), P(("date", "path"), None)),
        check_vma=False,
    )
```

```python
import jax
import jax.numpy as jnp
from jax import lax
from jax.experimental import pallas as pl
from jax.experimental.pallas import tpu as pltpu
from jax.sharding import PartitionSpec as P

F32 = jnp.float32
BF16 = jnp.bfloat16
BLOCK = 256
META_ROWS = 8


def margin_terms(arrived, got_codes, risk_weights, correlation, funding_spread):
    path_rows = arrived.shape[0]
    cpty_count = funding_spread.shape[0]
    bucket_count = risk_weights.shape[0]
    is_filled = got_codes >= 0
    column_ids = jnp.arange(cpty_count * bucket_count, dtype=jnp.int32)
    hot_table = (got_codes[:, None] == column_ids[None, :]).astype(jnp.bfloat16)
    bucket_sums = jnp.dot(arrived, hot_table, preferred_element_type=jnp.float32)
    weighted = (
        bucket_sums.reshape(path_rows, cpty_count, bucket_count) * risk_weights[None, None, :]
    )
    rho_w = jnp.einsum("pcb,db->pcd", weighted, correlation, precision=lax.Precision.HIGHEST)
    margin_now = jnp.sqrt(jnp.sum(weighted * rho_w, axis=2) + 1e-06)
    sens_bar = (
        funding_spread[None, :, None] * risk_weights[None, None, :] * rho_w / margin_now[:, :, None]
    )
    flat_bar = sens_bar.reshape(path_rows, cpty_count * bucket_count)
    safe_codes = jnp.where(is_filled, got_codes, 0)
    slot_bar = jnp.take(flat_bar, safe_codes, axis=1) * is_filled[None, :].astype(jnp.float32)
    return (margin_now, slot_bar.astype(jnp.bfloat16))


def exchange_body(
    basis_values, coefficients, trade_cpty, trade_bucket, risk_weights, correlation, funding_spread
):
    owners = lax.axis_size("trade")
    per_device = coefficients.shape[0]
    capacity = max(2, 2 * per_device // owners)
    slot_total = owners * capacity
    cpty_count = funding_spread.shape[0]
    bucket_count = risk_weights.shape[0]
    path_rows = basis_values.shape[0]
    owner_of = trade_cpty // cpty_count
    trade_code = trade_cpty % cpty_count * bucket_count + trade_bucket
    position = jnp.arange(per_device, dtype=jnp.int32)
    same_owner = owner_of[:, None] == owner_of[None, :]
    earlier = position[None, :] < position[:, None]
    rank_in = jnp.sum((same_owner & earlier).astype(jnp.int32), axis=1)
    slot_index = owner_of * capacity + rank_in
    codes_out = jnp.full((slot_total,), -1, jnp.int32).at[slot_index].set(trade_code)
    got_codes = lax.all_to_all(codes_out, "trade", split_axis=0, concat_axis=0, tiled=True)
    delta_rows = lax.dot_general(
        basis_values, coefficients, (((1,), (1,)), ((), ())), preferred_element_type=jnp.float32
    ).astype(jnp.bfloat16)
    outgoing = jnp.zeros((path_rows, slot_total), jnp.bfloat16).at[:, slot_index].set(delta_rows)
    arrived = lax.all_to_all(outgoing, "trade", split_axis=1, concat_axis=1, tiled=True)
    margin_now, slot_bar = margin_terms(
        arrived, got_codes, risk_weights, correlation, funding_spread
    )
    returned = lax.all_to_all(slot_bar, "trade", split_axis=1, concat_axis=1, tiled=True)
    delta_bar = returned[:, slot_index]
    partial_adj = jnp.dot(delta_bar, coefficients, preferred_element_type=jnp.float32)
    basis_adjoint = lax.psum(partial_adj, "trade").astype(jnp.bfloat16)
    return (margin_now.T, basis_adjoint)


def dot(a, b):
    return jnp.dot(a, b, preferred_element_type=F32)


def split(x):
    hi = x.astype(BF16)
    return hi, (x - hi.astype(F32)).astype(BF16)


def one_hot_t(row, count):
    ids = lax.broadcasted_iota(jnp.int32, (count, row.shape[1]), 0).astype(F32)
    return (ids == row).astype(F32).astype(BF16)


def pack_kernel(cpty_ref, bucket_ref, spread_ref, coef_ref, out_ref, meta, *, cpties):
    per = coef_ref.shape[0]
    rows = meta.shape[0]
    cpty = cpty_ref[...]
    owner = cpty // cpties
    meta[...] = jnp.zeros_like(meta)
    meta[0:1, :per] = owner.astype(F32)
    meta[1:2, :per] = (cpty - owner * cpties).astype(F32)
    meta[2:3, :per] = bucket_ref[...].astype(F32)
    spread = spread_ref[...]
    high = spread.astype(BF16).astype(F32)
    middle = (spread - high).astype(BF16).astype(F32)
    meta[3:4, :cpties] = high
    meta[4:5, :cpties] = middle
    meta[5:6, :cpties] = spread - high - middle
    out_ref[:per] = coef_ref[...]
    out_ref[per : per + rows] = meta[...].astype(BF16)


def all_trades_kernel(basis_ref, weight_ref, corr_ref, *refs, shards, per, cpties):
    both, ends = refs[: shards - 1], refs[shards - 1 : shards + 1]
    margin_ref, adj_ref = refs[shards + 1 : shards + 3]
    basis, coef, tails, meta, spread, delta, m_hi, m_lo, r_all, bar, sem = refs[shards + 3 :]
    trades = shards * per
    groups = shards * cpties
    buckets = corr_ref.shape[0]
    me, core = lax.axis_index("trade"), lax.axis_index("path")

    def shard_copies(s, ref):
        head = pltpu.make_async_copy(
            ref.at[pl.ds(per, META_ROWS)], tails.at[pl.ds(s * META_ROWS, META_ROWS)], sem.at[s]
        )
        body = pltpu.make_async_copy(
            ref.at[pl.ds(0, per)], coef.at[pl.ds(s * per, per)], sem.at[shards + s]
        )
        return head, body

    heads, copies = [], []
    for s, ref in enumerate(both):
        head, body = shard_copies(s, ref)
        head.start()
        body.start()
        heads.append(head)
        copies.append(body)
    for k in range(1):
        s = len(both) + k
        for side in range(2):

            @pl.when(core == side)
            def _():
                for copy in shard_copies(s, ends[2 * k + side]):
                    copy.start()

        head, body = shard_copies(s, ends[2 * k])
        heads.append(head)
        copies.append(body)
    copies.append(pltpu.make_async_copy(basis_ref, basis, sem.at[2 * shards]))
    copies[-1].start()
    for copy in heads:
        copy.wait()
    for s in range(shards):
        tail = tails[s * META_ROWS : (s + 1) * META_ROWS, :].astype(F32)
        meta[:, s * per : (s + 1) * per] = tail[:, :per]
        spread[:, s * cpties : (s + 1) * cpties] = (
            tail[3:4, :cpties] + tail[4:5, :cpties] + tail[5:6, :cpties]
        )
    offset = meta[0:1, :].astype(jnp.int32) ^ me
    group = meta[1:2, :]
    for s in range(1, shards):
        there = jnp.where(core == 0, LAYOUT[0][s], LAYOUT[1][s])
        group = group + jnp.where(offset == there, F32(s * cpties), F32(0))
    bucket = meta[2:3, :]
    group_t = one_hot_t(group, groups)
    group_hot = group_t.T
    bucket_t = one_hot_t(bucket, buckets)
    bucket_hot = bucket_t.T
    weight = weight_ref[...]
    weight_col = jnp.broadcast_to(weight, (buckets, buckets)).T
    c_hi, c_lo = split(corr_ref[...] * weight * weight_col)
    gathered = jnp.concatenate(
        [dot(c_hi, bucket_t).astype(BF16), dot(c_lo, bucket_t).astype(BF16)], 0
    )
    bucket_two = jnp.concatenate([bucket_hot, bucket_hot], 1)
    group_col = jnp.broadcast_to(group, (groups, trades)).T[:, :1]
    blocks = [slice(k, min(k + BLOCK, trades)) for k in range(0, trades, BLOCK)]
    for cols in blocks:
        for rows in blocks:
            pair = dot(bucket_two[rows], gathered[:, cols])
            pair = jnp.where(group_col[rows] == group[:, cols], pair, 0.0)
            hi, lo = split(pair)
            m_hi[rows, cols] = hi
            m_lo[rows, cols] = lo
    for copy in copies:
        copy.wait()
    for cols in blocks:
        delta[:, cols] = lax.dot_general(
            basis[...], coef[cols, :], (((1,), (1,)), ((), ())), preferred_element_type=F32
        ).astype(BF16)
    for cols in blocks:
        r_all[:, cols] = dot(delta[...], m_hi[:, cols]) + dot(delta[...], m_lo[:, cols])
    squares = None
    for cols in blocks:
        hi, lo = split(delta[:, cols].astype(F32) * r_all[:, cols])
        part = dot(hi, group_hot[cols]) + dot(lo, group_hot[cols])
        squares = part if squares is None else squares + part
    margin = jnp.sqrt(squares + 1e-06)
    margin_ref[...] = margin.T[:cpties]
    hi, lo = split(spread[...] / margin)
    scale = jnp.concatenate([hi, lo], 1)
    group_two = jnp.concatenate([group_t, group_t], 0)
    for cols in blocks:
        bar[:, cols] = (r_all[:, cols] * dot(scale, group_two[:, cols])).astype(BF16)
    adj_ref[...] = dot(bar[...], coef[...]).astype(BF16)


def swap_cores(x):
    return lax.ppermute(x, "path", [(0, 1), (1, 0)])


def fetch(x, owners, *offsets):
    pairs = []
    for core, offset in enumerate(offsets):
        pairs += [((i ^ offset) * 2 + core, i * 2 + core) for i in range(owners)]
    return lax.ppermute(x, ("trade", "path"), pairs)


LAYOUT = ((0, 4, 2, 5, 3, 6, 7, 1), (0, 2, 4, 3, 5, 7, 6, 1))


def gather_shards(x, owners):
    first = fetch(x, owners, 4, 2)
    beside = fetch(x, owners, 0, 1)
    beside, first = lax.optimization_barrier((beside, first))
    first_other = swap_cores(first)
    second = fetch(first, owners, 1, 1)
    opposite = jnp.where(lax.axis_index("path") == 0, first, first_other)
    third = fetch(opposite, owners, 2, 3)
    both = [x, first, first_other, second, swap_cores(second), third, swap_cores(third)]
    return both + [swap_cores(beside), beside]


def gather_body(
    basis_values, coefficients, trade_cpty, trade_bucket, risk_weights, correlation, funding_spread
):
    owners = lax.axis_size("trade")
    per = coefficients.shape[0]
    cpties = funding_spread.shape[0]
    buckets = risk_weights.shape[0]
    paths, width = basis_values.shape
    trades = owners * per
    vmem = pl.BlockSpec(memory_space=pltpu.VMEM)
    anywhere = pl.BlockSpec(memory_space=pl.ANY)

    def pack(*refs):
        pack_kernel(*refs, cpties=cpties)

    payload = pl.pallas_call(
        pack,
        out_shape=jax.ShapeDtypeStruct((per + META_ROWS, width), BF16),
        in_specs=[vmem] * 4,
        out_specs=vmem,
        scratch_shapes=[pltpu.VMEM((META_ROWS, width), F32)],
    )(
        trade_cpty.reshape(1, per),
        trade_bucket.reshape(1, per),
        funding_spread.reshape(1, cpties),
        coefficients,
    )
    gathered = gather_shards(payload, owners)

    def kernel(*refs):
        all_trades_kernel(*refs, shards=owners, per=per, cpties=cpties)

    return pl.pallas_call(
        kernel,
        out_shape=[
            jax.ShapeDtypeStruct((cpties, paths), F32),
            jax.ShapeDtypeStruct((paths, width), BF16),
        ],
        in_specs=[pl.BlockSpec(memory_space=pltpu.HBM), vmem, vmem]
        + [anywhere] * len(gathered),
        out_specs=[vmem, vmem],
        scratch_shapes=[
            pltpu.VMEM((paths, width), BF16),
            pltpu.VMEM((trades, width), BF16),
            pltpu.VMEM((owners * META_ROWS, width), BF16),
            pltpu.VMEM((META_ROWS, trades), F32),
            pltpu.VMEM((1, owners * cpties), F32),
            pltpu.VMEM((paths, trades), BF16),
            pltpu.VMEM((trades, trades), BF16),
            pltpu.VMEM((trades, trades), BF16),
            pltpu.VMEM((paths, trades), F32),
            pltpu.VMEM((paths, trades), BF16),
            pltpu.SemaphoreType.DMA((2 * owners + 1,)),
        ],
        compiler_params=pltpu.CompilerParams(vmem_limit_bytes=40 << 20),
    )(basis_values, risk_weights.reshape(1, buckets), correlation, *gathered)


def solution(mesh):
    placed = (
        P(("date", "path"), None),
        P(("date", "trade"), None),
        P("trade"),
        P("trade"),
        P(),
        P(),
        P("trade"),
    )
    small = mesh.shape["trade"] == 8 and mesh.shape["path"] == 2
    return jax.shard_map(
        gather_body if small else exchange_body,
        mesh=mesh,
        in_specs=placed,
        out_specs=(P("trade", ("date", "path")), P(("date", "path"), None)),
        check_vma=False,
    )
```

```python
import jax
import jax.numpy as jnp
from jax import lax
from jax.experimental import pallas as pl
from jax.experimental.pallas import tpu as pltpu
from jax.sharding import PartitionSpec as P

F32 = jnp.float32
BF16 = jnp.bfloat16
BLOCK = 256
META_ROWS = 8


def margin_terms(arrived, got_codes, risk_weights, correlation, funding_spread):
    path_rows = arrived.shape[0]
    cpty_count = funding_spread.shape[0]
    bucket_count = risk_weights.shape[0]
    is_filled = got_codes >= 0
    column_ids = jnp.arange(cpty_count * bucket_count, dtype=jnp.int32)
    hot_table = (got_codes[:, None] == column_ids[None, :]).astype(jnp.bfloat16)
    bucket_sums = jnp.dot(arrived, hot_table, preferred_element_type=jnp.float32)
    weighted = (
        bucket_sums.reshape(path_rows, cpty_count, bucket_count) * risk_weights[None, None, :]
    )
    rho_w = jnp.einsum("pcb,db->pcd", weighted, correlation, precision=lax.Precision.HIGHEST)
    margin_now = jnp.sqrt(jnp.sum(weighted * rho_w, axis=2) + 1e-06)
    sens_bar = (
        funding_spread[None, :, None] * risk_weights[None, None, :] * rho_w / margin_now[:, :, None]
    )
    flat_bar = sens_bar.reshape(path_rows, cpty_count * bucket_count)
    safe_codes = jnp.where(is_filled, got_codes, 0)
    slot_bar = jnp.take(flat_bar, safe_codes, axis=1) * is_filled[None, :].astype(jnp.float32)
    return (margin_now, slot_bar.astype(jnp.bfloat16))


def exchange_body(
    basis_values, coefficients, trade_cpty, trade_bucket, risk_weights, correlation, funding_spread
):
    owners = lax.axis_size("trade")
    per_device = coefficients.shape[0]
    capacity = max(2, 2 * per_device // owners)
    slot_total = owners * capacity
    cpty_count = funding_spread.shape[0]
    bucket_count = risk_weights.shape[0]
    path_rows = basis_values.shape[0]
    owner_of = trade_cpty // cpty_count
    trade_code = trade_cpty % cpty_count * bucket_count + trade_bucket
    position = jnp.arange(per_device, dtype=jnp.int32)
    same_owner = owner_of[:, None] == owner_of[None, :]
    earlier = position[None, :] < position[:, None]
    rank_in = jnp.sum((same_owner & earlier).astype(jnp.int32), axis=1)
    slot_index = owner_of * capacity + rank_in
    codes_out = jnp.full((slot_total,), -1, jnp.int32).at[slot_index].set(trade_code)
    got_codes = lax.all_to_all(codes_out, "trade", split_axis=0, concat_axis=0, tiled=True)
    delta_rows = lax.dot_general(
        basis_values, coefficients, (((1,), (1,)), ((), ())), preferred_element_type=jnp.float32
    ).astype(jnp.bfloat16)
    outgoing = jnp.zeros((path_rows, slot_total), jnp.bfloat16).at[:, slot_index].set(delta_rows)
    arrived = lax.all_to_all(outgoing, "trade", split_axis=1, concat_axis=1, tiled=True)
    margin_now, slot_bar = margin_terms(
        arrived, got_codes, risk_weights, correlation, funding_spread
    )
    returned = lax.all_to_all(slot_bar, "trade", split_axis=1, concat_axis=1, tiled=True)
    delta_bar = returned[:, slot_index]
    partial_adj = jnp.dot(delta_bar, coefficients, preferred_element_type=jnp.float32)
    basis_adjoint = lax.psum(partial_adj, "trade").astype(jnp.bfloat16)
    return (margin_now.T, basis_adjoint)


def dot(a, b):
    return jnp.dot(a, b, preferred_element_type=F32)


def split(x):
    hi = x.astype(BF16)
    return hi, (x - hi.astype(F32)).astype(BF16)


def one_hot_t(row, count):
    ids = lax.broadcasted_iota(jnp.int32, (count, row.shape[1]), 0).astype(F32)
    return (ids == row).astype(F32).astype(BF16)


def pack_kernel(*refs, cpties):
    sources, out_ref, scratch, sem = refs[:4], refs[4], refs[5:8], refs[8]
    per, width = sources[3].shape
    goals = (*scratch, out_ref.at[pl.ds(0, per)])
    copies = [pltpu.make_async_copy(s, g, sem.at[k]) for k, (s, g) in enumerate(zip(sources, goals))]
    for copy in copies:
        copy.start()
    for copy in copies[:3]:
        copy.wait()
    cpty, bucket, spread = (ref[...] for ref in scratch)
    owner = cpty // cpties
    high = spread.astype(BF16).astype(F32)
    middle = (spread - high).astype(BF16).astype(F32)
    rows = [owner, cpty - owner * cpties, bucket, high, middle, spread - high - middle]
    out_ref[per:] = jnp.zeros((META_ROWS, width), BF16)
    for k, row in enumerate(rows):
        out_ref[per + k : per + k + 1, : row.shape[1]] = row.astype(F32).astype(BF16)
    copies[3].wait()


def cut(start, stop):
    return [slice(k, min(k + BLOCK, stop)) for k in range(start, stop, BLOCK)]


def deltas(basis, coef, rows):
    return lax.dot_general(
        basis[...], coef[rows, :], (((1,), (1,)), ((), ())), preferred_element_type=F32
    ).astype(BF16)


def place_shards(coef, sides, both, core, per):
    spots = [s for s in range(len(both) + 1) if s != EITHER]
    for s, ref in zip(spots, both):
        coef[s * per : (s + 1) * per] = ref[:per]
    for side, ref in enumerate(sides):

        @pl.when(core == side)
        def _():
            coef[EITHER * per : (EITHER + 1) * per] = ref[:per]


def read_meta(tails, meta, spread, per, cpties):
    for s, tail in enumerate(tails):
        meta[:, s * per : (s + 1) * per] = tail[:, :per]
        spread[:, s * cpties : (s + 1) * cpties] = (
            tail[3:4, :cpties] + tail[4:5, :cpties] + tail[5:6, :cpties]
        )


def shard_tails(sides, both, core, per):
    tails = [ref[per : per + META_ROWS].astype(F32) for ref in both]
    zero, one = (ref[per : per + META_ROWS].astype(F32) for ref in sides)
    tails.insert(EITHER, jnp.where(core == 0, zero, one))
    return tails


def groups_of(meta, me, core, cpties):
    offset = meta[0:1, :].astype(jnp.int32) ^ me
    group = meta[1:2, :]
    for s in range(1, len(LAYOUT[0])):
        there = jnp.where(core == 0, LAYOUT[0][s], LAYOUT[1][s])
        group = group + jnp.where(offset == there, F32(s * cpties), F32(0))
    return group


def pair_factors(table, bucket_t):
    buckets = bucket_t.shape[0]
    bucket_hot = bucket_t.T
    right = [dot(table[k * buckets : (k + 1) * buckets], bucket_t).astype(BF16) for k in range(2)]
    return jnp.concatenate([bucket_hot, bucket_hot], 1), jnp.concatenate(right, 0)


def fill_pairs(left, right, group_col, group, m_hi, m_lo, rows, cols):
    pair = dot(left[rows], right[:, cols])
    pair = jnp.where(group_col[rows] == group[:, cols], pair, 0.0)
    m_hi[rows, cols], m_lo[rows, cols] = split(pair)


def column(row, lanes):
    return jnp.broadcast_to(row, (lanes, row.shape[1])).T[:, :1]


def early_kernel(basis_ref, weight_ref, corr_ref, *refs, per, cpties):
    sides, both = refs[:2], refs[2:5]
    delta, r_part, table = refs[5:8]
    basis, coef, weight, corr, meta, spread, m_hi, m_lo, sem = refs[8:]
    buckets = corr.shape[0]
    early = delta.shape[1]
    me, core = lax.axis_index("trade"), lax.axis_index("path")
    small = [
        pltpu.make_async_copy(weight_ref, weight, sem.at[0]),
        pltpu.make_async_copy(corr_ref, corr, sem.at[1]),
    ]
    whole = pltpu.make_async_copy(basis_ref, basis, sem.at[2])
    for copy in (*small, whole):
        copy.start()
    read_meta(shard_tails(sides, both, core, per), meta, spread, per, cpties)
    group = groups_of(meta[:, :early], me, core, cpties)
    bucket_t = one_hot_t(meta[2:3, :early], buckets)
    place_shards(coef, sides, both, core, per)
    for copy in small:
        copy.wait()
    weight_col = column(weight[...], buckets)
    hi, lo = split(corr[...] * weight[...] * weight_col)
    table[:buckets] = hi
    table[buckets:] = lo
    left, right = pair_factors(table, bucket_t)
    group_col = column(group, buckets)
    blocks = cut(0, early)
    for cols in blocks:
        for rows in blocks:
            fill_pairs(left, right, group_col, group, m_hi, m_lo, rows, cols)
    whole.wait()
    for cols in blocks:
        delta[:, cols] = deltas(basis, coef, cols)
    for cols in blocks:
        r_part[:, cols] = dot(delta[...], m_hi[:, cols]) + dot(delta[...], m_lo[:, cols])


def late_kernel(basis_ref, early_delta, r_part, table, *refs, per, cpties):
    shards = len(LAYOUT[0])
    sides, both = refs[:2], refs[2 : shards + 1]
    margin_ref, adj_ref = refs[shards + 1 : shards + 3]
    basis, coef, meta, spread, delta, m_hi, m_lo, r_all, bar, sem = refs[shards + 3 :]
    early = early_delta.shape[1]
    trades = coef.shape[0]
    groups = spread.shape[1]
    buckets = table.shape[0] // 2
    me, core = lax.axis_index("trade"), lax.axis_index("path")
    whole = pltpu.make_async_copy(basis_ref, basis, sem.at[0])
    whole.start()
    read_meta(shard_tails(sides, both, core, per), meta, spread, per, cpties)
    group = groups_of(meta, me, core, cpties)
    group_t = one_hot_t(group, groups)
    group_hot = group_t.T
    left, right = pair_factors(table, one_hot_t(meta[2:3, :], buckets))
    group_col = column(group, groups)
    place_shards(coef, sides, both, core, per)
    blocks = cut(0, trades)

    def fill(cols):
        for rows in blocks if cols.start >= early else cut(early, trades):
            fill_pairs(left, right, group_col, group, m_hi, m_lo, rows, cols)

    whole.wait()
    delta[:, :early] = early_delta[...]
    for cols in cut(early, trades):
        delta[:, cols] = deltas(basis, coef, cols)
    fill(blocks[0])
    for k, cols in enumerate(blocks):
        if k + 1 < len(blocks):
            fill(blocks[k + 1])
        if cols.start >= early:
            r_all[:, cols] = dot(delta[...], m_hi[:, cols]) + dot(delta[...], m_lo[:, cols])
        else:
            late = dot(delta[:, early:], m_hi[early:, cols]) + dot(delta[:, early:], m_lo[early:, cols])
            r_all[:, cols] = r_part[:, cols] + late
    squares = None
    for cols in blocks:
        hi, lo = split(delta[:, cols].astype(F32) * r_all[:, cols])
        part = dot(hi, group_hot[cols]) + dot(lo, group_hot[cols])
        squares = part if squares is None else squares + part
    margin = jnp.sqrt(squares + 1e-06)
    margin_ref[...] = margin.T[:cpties]
    hi, lo = split(spread[...] / margin)
    scale = jnp.concatenate([hi, lo], 1)
    group_two = jnp.concatenate([group_t, group_t], 0)
    for cols in blocks:
        bar[:, cols] = (r_all[:, cols] * dot(scale, group_two[:, cols])).astype(BF16)
    adj_ref[...] = dot(bar[...], coef[...]).astype(BF16)


def swap_cores(x):
    return lax.ppermute(x, "path", [(0, 1), (1, 0)])


def fetch(x, owners, *offsets):
    pairs = []
    for core, offset in enumerate(offsets):
        pairs += [((i ^ offset) * 2 + core, i * 2 + core) for i in range(owners)]
    return lax.ppermute(x, ("trade", "path"), pairs)


LAYOUT = ((0, 4, 2, 1, 5, 3, 6, 7), (0, 2, 4, 1, 3, 5, 7, 6))
EITHER = 3


def hold(x):
    return pltpu.with_memory_space_constraint(x, pltpu.HBM)


def gather_body(
    basis_values, coefficients, trade_cpty, trade_bucket, risk_weights, correlation, funding_spread
):
    owners = lax.axis_size("trade")
    per = coefficients.shape[0]
    cpties = funding_spread.shape[0]
    buckets = risk_weights.shape[0]
    paths, width = basis_values.shape
    trades = owners * per
    vmem = pl.BlockSpec(memory_space=pltpu.VMEM)
    anywhere = pl.BlockSpec(memory_space=pl.ANY)

    def pack(*refs):
        pack_kernel(*refs, cpties=cpties)

    payload = pl.pallas_call(
        pack,
        out_shape=jax.ShapeDtypeStruct((per + META_ROWS, width), BF16),
        in_specs=[anywhere] * 4,
        out_specs=vmem,
        scratch_shapes=[
            pltpu.VMEM((1, per), jnp.int32),
            pltpu.VMEM((1, per), jnp.int32),
            pltpu.VMEM((1, cpties), F32),
            pltpu.SemaphoreType.DMA((4,)),
        ],
        compiler_params=pltpu.CompilerParams(vmem_limit_bytes=4 << 20),
    )(
        hold(trade_cpty.reshape(1, per)),
        hold(trade_bucket.reshape(1, per)),
        hold(funding_spread.reshape(1, cpties)),
        hold(coefficients),
    )
    core = lax.axis_index("path")
    first = fetch(payload, owners, 4, 2)
    beside = fetch(payload, owners, 0, 1)
    beside, first = lax.optimization_barrier((beside, first))
    sent = jnp.where(core == 0, first, beside)
    second = fetch(sent, owners, 1, 2)
    first_other = swap_cores(first)
    _, first_other = lax.optimization_barrier((sent, first_other))
    opposite = jnp.where(core == 0, first, first_other)
    third = fetch(opposite, owners, 2, 3)
    present = (swap_cores(beside), beside, payload, first, first_other)
    early_trades = trades // 2 // BLOCK * BLOCK
    groups = owners * cpties

    def early(*refs):
        early_kernel(*refs, per=per, cpties=cpties)

    state = pl.pallas_call(
        early,
        out_shape=[
            jax.ShapeDtypeStruct((paths, early_trades), BF16),
            jax.ShapeDtypeStruct((paths, early_trades), F32),
            jax.ShapeDtypeStruct((2 * buckets, buckets), BF16),
        ],
        in_specs=[anywhere] * 3 + [vmem] * len(present),
        out_specs=[vmem] * 3,
        scratch_shapes=[
            pltpu.VMEM((paths, width), BF16),
            pltpu.VMEM((trades // 2, width), BF16),
            pltpu.VMEM((1, buckets), F32),
            pltpu.VMEM((buckets, buckets), F32),
            pltpu.VMEM((META_ROWS, trades // 2), F32),
            pltpu.VMEM((1, groups // 2), F32),
            pltpu.VMEM((early_trades, early_trades), BF16),
            pltpu.VMEM((early_trades, early_trades), BF16),
            pltpu.SemaphoreType.DMA((3,)),
        ],
        cost_estimate=pl.CostEstimate(flops=2 * 10**9, bytes_accessed=4 * 10**6, transcendentals=0),
        compiler_params=pltpu.CompilerParams(vmem_limit_bytes=16 << 20),
    )(
        hold(basis_values),
        hold(risk_weights.reshape(1, buckets)),
        hold(correlation),
        *present,
    )
    second, *state = lax.optimization_barrier((second, *state))
    shards = present + (second, swap_cores(second), third, swap_cores(third))

    def late(*refs):
        late_kernel(*refs, per=per, cpties=cpties)

    return pl.pallas_call(
        late,
        out_shape=[
            jax.ShapeDtypeStruct((cpties, paths), F32),
            jax.ShapeDtypeStruct((paths, width), BF16),
        ],
        in_specs=[anywhere] + [vmem] * (len(state) + len(shards)),
        out_specs=[vmem, vmem],
        scratch_shapes=[
            pltpu.VMEM((paths, width), BF16),
            pltpu.VMEM((trades, width), BF16),
            pltpu.VMEM((META_ROWS, trades), F32),
            pltpu.VMEM((1, groups), F32),
            pltpu.VMEM((paths, trades), BF16),
            pltpu.VMEM((trades, trades), BF16),
            pltpu.VMEM((trades, trades), BF16),
            pltpu.VMEM((paths, trades), F32),
            pltpu.VMEM((paths, trades), BF16),
            pltpu.SemaphoreType.DMA((1,)),
        ],
        compiler_params=pltpu.CompilerParams(vmem_limit_bytes=36 << 20),
    )(hold(basis_values), *state, *shards)


def solution(mesh):
    placed = (
        P(("date", "path"), None),
        P(("date", "trade"), None),
        P("trade"),
        P("trade"),
        P(),
        P(),
        P("trade"),
    )
    small = mesh.shape["trade"] == 8 and mesh.shape["path"] == 2
    return jax.shard_map(
        gather_body if small else exchange_body,
        mesh=mesh,
        in_specs=placed,
        out_specs=(P("trade", ("date", "path")), P(("date", "path"), None)),
        check_vma=False,
    )
```

```python
import jax
import jax.numpy as jnp
from jax import lax
from jax.experimental import pallas as pl
from jax.experimental.pallas import tpu as pltpu
from jax.sharding import PartitionSpec as P

F32 = jnp.float32
BF16 = jnp.bfloat16
BLOCK = 256
META_ROWS = 8


def margin_terms(arrived, got_codes, risk_weights, correlation, funding_spread):
    path_rows = arrived.shape[0]
    cpty_count = funding_spread.shape[0]
    bucket_count = risk_weights.shape[0]
    is_filled = got_codes >= 0
    column_ids = jnp.arange(cpty_count * bucket_count, dtype=jnp.int32)
    hot_table = (got_codes[:, None] == column_ids[None, :]).astype(jnp.bfloat16)
    bucket_sums = jnp.dot(arrived, hot_table, preferred_element_type=jnp.float32)
    weighted = (
        bucket_sums.reshape(path_rows, cpty_count, bucket_count) * risk_weights[None, None, :]
    )
    rho_w = jnp.einsum("pcb,db->pcd", weighted, correlation, precision=lax.Precision.HIGHEST)
    margin_now = jnp.sqrt(jnp.sum(weighted * rho_w, axis=2) + 1e-06)
    sens_bar = (
        funding_spread[None, :, None] * risk_weights[None, None, :] * rho_w / margin_now[:, :, None]
    )
    flat_bar = sens_bar.reshape(path_rows, cpty_count * bucket_count)
    safe_codes = jnp.where(is_filled, got_codes, 0)
    slot_bar = jnp.take(flat_bar, safe_codes, axis=1) * is_filled[None, :].astype(jnp.float32)
    return (margin_now, slot_bar.astype(jnp.bfloat16))


def exchange_body(
    basis_values, coefficients, trade_cpty, trade_bucket, risk_weights, correlation, funding_spread
):
    owners = lax.axis_size("trade")
    per_device = coefficients.shape[0]
    capacity = max(2, 2 * per_device // owners)
    slot_total = owners * capacity
    cpty_count = funding_spread.shape[0]
    bucket_count = risk_weights.shape[0]
    path_rows = basis_values.shape[0]
    owner_of = trade_cpty // cpty_count
    trade_code = trade_cpty % cpty_count * bucket_count + trade_bucket
    position = jnp.arange(per_device, dtype=jnp.int32)
    same_owner = owner_of[:, None] == owner_of[None, :]
    earlier = position[None, :] < position[:, None]
    rank_in = jnp.sum((same_owner & earlier).astype(jnp.int32), axis=1)
    slot_index = owner_of * capacity + rank_in
    codes_out = jnp.full((slot_total,), -1, jnp.int32).at[slot_index].set(trade_code)
    got_codes = lax.all_to_all(codes_out, "trade", split_axis=0, concat_axis=0, tiled=True)
    delta_rows = lax.dot_general(
        basis_values, coefficients, (((1,), (1,)), ((), ())), preferred_element_type=jnp.float32
    ).astype(jnp.bfloat16)
    outgoing = jnp.zeros((path_rows, slot_total), jnp.bfloat16).at[:, slot_index].set(delta_rows)
    arrived = lax.all_to_all(outgoing, "trade", split_axis=1, concat_axis=1, tiled=True)
    margin_now, slot_bar = margin_terms(
        arrived, got_codes, risk_weights, correlation, funding_spread
    )
    returned = lax.all_to_all(slot_bar, "trade", split_axis=1, concat_axis=1, tiled=True)
    delta_bar = returned[:, slot_index]
    partial_adj = jnp.dot(delta_bar, coefficients, preferred_element_type=jnp.float32)
    basis_adjoint = lax.psum(partial_adj, "trade").astype(jnp.bfloat16)
    return (margin_now.T, basis_adjoint)


def dot(a, b):
    return jnp.dot(a, b, preferred_element_type=F32)


def split(x):
    hi = x.astype(BF16)
    return hi, (x - hi.astype(F32)).astype(BF16)


def one_hot_t(row, count):
    ids = lax.broadcasted_iota(jnp.int32, (count, row.shape[1]), 0).astype(F32)
    return (ids == row).astype(F32).astype(BF16)


def pack_kernel(*refs, cpties):
    sources, out_ref, scratch, sem = refs[:4], refs[4], refs[5:8], refs[8]
    per, width = sources[3].shape
    goals = (*scratch, out_ref.at[pl.ds(0, per)])
    copies = [pltpu.make_async_copy(s, g, sem.at[k]) for k, (s, g) in enumerate(zip(sources, goals))]
    for copy in copies:
        copy.start()
    for copy in copies[:3]:
        copy.wait()
    cpty, bucket, spread = (ref[...] for ref in scratch)
    owner = cpty // cpties
    high = spread.astype(BF16).astype(F32)
    middle = (spread - high).astype(BF16).astype(F32)
    rows = [owner, cpty - owner * cpties, bucket, high, middle, spread - high - middle]
    out_ref[per:] = jnp.zeros((META_ROWS, width), BF16)
    for k, row in enumerate(rows):
        out_ref[per + k : per + k + 1, : row.shape[1]] = row.astype(F32).astype(BF16)
    copies[3].wait()


def cut(start, stop):
    return [slice(k, min(k + BLOCK, stop)) for k in range(start, stop, BLOCK)]


def deltas(basis, coef, rows):
    return lax.dot_general(
        basis[...], coef[rows, :], (((1,), (1,)), ((), ())), preferred_element_type=F32
    ).astype(BF16)


def place_shards(coef, sides, both, core, per):
    spots = [s for s in range(len(both) + 1) if s != EITHER]
    for s, ref in zip(spots, both):
        coef[s * per : (s + 1) * per] = ref[:per]
    for side, ref in enumerate(sides):

        @pl.when(core == side)
        def _():
            coef[EITHER * per : (EITHER + 1) * per] = ref[:per]


def read_meta(tails, meta, spread, per, cpties):
    for s, tail in enumerate(tails):
        meta[:, s * per : (s + 1) * per] = tail[:, :per]
        spread[:, s * cpties : (s + 1) * cpties] = (
            tail[3:4, :cpties] + tail[4:5, :cpties] + tail[5:6, :cpties]
        )


def shard_tails(sides, both, core, per):
    tails = [ref[per : per + META_ROWS].astype(F32) for ref in both]
    zero, one = (ref[per : per + META_ROWS].astype(F32) for ref in sides)
    tails.insert(EITHER, jnp.where(core == 0, zero, one))
    return tails


def groups_of(meta, me, core, cpties):
    offset = meta[0:1, :].astype(jnp.int32) ^ me
    group = meta[1:2, :]
    for s in range(1, len(LAYOUT[0])):
        there = jnp.where(core == 0, LAYOUT[0][s], LAYOUT[1][s])
        group = group + jnp.where(offset == there, F32(s * cpties), F32(0))
    return group


def pair_factors(table, bucket_t):
    buckets = bucket_t.shape[0]
    bucket_hot = bucket_t.T
    right = [dot(table[k * buckets : (k + 1) * buckets], bucket_t).astype(BF16) for k in range(2)]
    return jnp.concatenate([bucket_hot, bucket_hot], 1), jnp.concatenate(right, 0)


def fill_pairs(left, right, group_col, group, m_hi, m_lo, rows, cols):
    pair = dot(left[rows], right[:, cols])
    pair = jnp.where(group_col[rows] == group[:, cols], pair, 0.0)
    m_hi[rows, cols], m_lo[rows, cols] = split(pair)


def column(row, lanes):
    return jnp.broadcast_to(row, (lanes, row.shape[1])).T[:, :1]


def early_kernel(basis_ref, weight_ref, corr_ref, *refs, per, cpties):
    sides, both = refs[:2], refs[2:5]
    delta, r_part, table, basis = refs[5:9]
    coef, weight, corr, meta, spread, m_hi, m_lo, sem = refs[9:]
    buckets = corr.shape[0]
    early = delta.shape[1]
    me, core = lax.axis_index("trade"), lax.axis_index("path")
    small = [
        pltpu.make_async_copy(weight_ref, weight, sem.at[0]),
        pltpu.make_async_copy(corr_ref, corr, sem.at[1]),
    ]
    whole = pltpu.make_async_copy(basis_ref, basis, sem.at[2])
    for copy in (*small, whole):
        copy.start()
    read_meta(shard_tails(sides, both, core, per), meta, spread, per, cpties)
    group = groups_of(meta[:, :early], me, core, cpties)
    bucket_t = one_hot_t(meta[2:3, :early], buckets)
    place_shards(coef, sides, both, core, per)
    for copy in small:
        copy.wait()
    weight_col = column(weight[...], buckets)
    hi, lo = split(corr[...] * weight[...] * weight_col)
    table[:buckets] = hi
    table[buckets:] = lo
    left, right = pair_factors(table, bucket_t)
    group_col = column(group, buckets)
    blocks = cut(0, early)
    for cols in blocks:
        for rows in blocks:
            fill_pairs(left, right, group_col, group, m_hi, m_lo, rows, cols)
    whole.wait()
    for cols in blocks:
        delta[:, cols] = deltas(basis, coef, cols)
    for cols in blocks:
        r_part[:, cols] = dot(delta[...], m_hi[:, cols]) + dot(delta[...], m_lo[:, cols])


def late_kernel(early_delta, r_part, table, basis, *refs, per, cpties):
    shards = len(LAYOUT[0])
    sides, both = refs[:2], refs[2 : shards + 1]
    margin_ref, adj_ref = refs[shards + 1 : shards + 3]
    coef, meta, spread, delta, m_hi, m_lo, r_all, bar = refs[shards + 3 :]
    early = early_delta.shape[1]
    trades = coef.shape[0]
    groups = spread.shape[1]
    buckets = table.shape[0] // 2
    me, core = lax.axis_index("trade"), lax.axis_index("path")
    read_meta(shard_tails(sides, both, core, per), meta, spread, per, cpties)
    group = groups_of(meta, me, core, cpties)
    group_t = one_hot_t(group, groups)
    group_hot = group_t.T
    left, right = pair_factors(table, one_hot_t(meta[2:3, :], buckets))
    group_col = column(group, groups)
    place_shards(coef, sides, both, core, per)
    blocks = cut(0, trades)

    def fill(cols):
        for rows in blocks if cols.start >= early else cut(early, trades):
            fill_pairs(left, right, group_col, group, m_hi, m_lo, rows, cols)

    delta[:, :early] = early_delta[...]
    for cols in cut(early, trades):
        delta[:, cols] = deltas(basis, coef, cols)
    fill(blocks[0])
    for k, cols in enumerate(blocks):
        if k + 1 < len(blocks):
            fill(blocks[k + 1])
        if cols.start >= early:
            r_all[:, cols] = dot(delta[...], m_hi[:, cols]) + dot(delta[...], m_lo[:, cols])
        else:
            late = dot(delta[:, early:], m_hi[early:, cols]) + dot(delta[:, early:], m_lo[early:, cols])
            r_all[:, cols] = r_part[:, cols] + late
    squares = None
    for cols in blocks:
        hi, lo = split(delta[:, cols].astype(F32) * r_all[:, cols])
        part = dot(hi, group_hot[cols]) + dot(lo, group_hot[cols])
        squares = part if squares is None else squares + part
    margin = jnp.sqrt(squares + 1e-06)
    margin_ref[...] = margin.T[:cpties]
    hi, lo = split(spread[...] / margin)
    scale = jnp.concatenate([hi, lo], 1)
    group_two = jnp.concatenate([group_t, group_t], 0)
    for cols in blocks:
        bar[:, cols] = (r_all[:, cols] * dot(scale, group_two[:, cols])).astype(BF16)
    adj_ref[...] = dot(bar[...], coef[...]).astype(BF16)


def swap_cores(x):
    return lax.ppermute(x, "path", [(0, 1), (1, 0)])


def fetch(x, owners, *offsets):
    pairs = []
    for core, offset in enumerate(offsets):
        pairs += [((i ^ offset) * 2 + core, i * 2 + core) for i in range(owners)]
    return lax.ppermute(x, ("trade", "path"), pairs)


LAYOUT = ((0, 4, 2, 1, 5, 3, 6, 7), (0, 2, 4, 1, 3, 5, 7, 6))
EITHER = 3


def hold(x):
    return pltpu.with_memory_space_constraint(x, pltpu.HBM)


def gather_body(
    basis_values, coefficients, trade_cpty, trade_bucket, risk_weights, correlation, funding_spread
):
    owners = lax.axis_size("trade")
    per = coefficients.shape[0]
    cpties = funding_spread.shape[0]
    buckets = risk_weights.shape[0]
    paths, width = basis_values.shape
    trades = owners * per
    vmem = pl.BlockSpec(memory_space=pltpu.VMEM)
    anywhere = pl.BlockSpec(memory_space=pl.ANY)

    def pack(*refs):
        pack_kernel(*refs, cpties=cpties)

    payload = pl.pallas_call(
        pack,
        out_shape=jax.ShapeDtypeStruct((per + META_ROWS, width), BF16),
        in_specs=[anywhere] * 4,
        out_specs=vmem,
        scratch_shapes=[
            pltpu.VMEM((1, per), jnp.int32),
            pltpu.VMEM((1, per), jnp.int32),
            pltpu.VMEM((1, cpties), F32),
            pltpu.SemaphoreType.DMA((4,)),
        ],
        compiler_params=pltpu.CompilerParams(vmem_limit_bytes=4 << 20),
    )(
        hold(trade_cpty.reshape(1, per)),
        hold(trade_bucket.reshape(1, per)),
        hold(funding_spread.reshape(1, cpties)),
        hold(coefficients),
    )
    core = lax.axis_index("path")
    first = fetch(payload, owners, 4, 2)
    beside = fetch(payload, owners, 0, 1)
    beside, first = lax.optimization_barrier((beside, first))
    sent = jnp.where(core == 0, first, beside)
    second = fetch(sent, owners, 1, 2)
    first_other = swap_cores(first)
    _, first_other = lax.optimization_barrier((sent, first_other))
    opposite = jnp.where(core == 0, first, first_other)
    third = fetch(opposite, owners, 2, 3)
    present = (swap_cores(beside), beside, payload, first, first_other)
    early_trades = trades // 2 // BLOCK * BLOCK
    groups = owners * cpties

    def early(*refs):
        early_kernel(*refs, per=per, cpties=cpties)

    state = pl.pallas_call(
        early,
        out_shape=[
            jax.ShapeDtypeStruct((paths, early_trades), BF16),
            jax.ShapeDtypeStruct((paths, early_trades), F32),
            jax.ShapeDtypeStruct((2 * buckets, buckets), BF16),
            jax.ShapeDtypeStruct((paths, width), BF16),
        ],
        in_specs=[anywhere] * 3 + [vmem] * len(present),
        out_specs=[vmem] * 4,
        scratch_shapes=[
            pltpu.VMEM((trades // 2, width), BF16),
            pltpu.VMEM((1, buckets), F32),
            pltpu.VMEM((buckets, buckets), F32),
            pltpu.VMEM((META_ROWS, trades // 2), F32),
            pltpu.VMEM((1, groups // 2), F32),
            pltpu.VMEM((early_trades, early_trades), BF16),
            pltpu.VMEM((early_trades, early_trades), BF16),
            pltpu.SemaphoreType.DMA((3,)),
        ],
        cost_estimate=pl.CostEstimate(flops=2 * 10**9, bytes_accessed=4 * 10**6, transcendentals=0),
        compiler_params=pltpu.CompilerParams(vmem_limit_bytes=16 << 20),
    )(
        hold(basis_values),
        hold(risk_weights.reshape(1, buckets)),
        hold(correlation),
        *present,
    )
    second, *state = lax.optimization_barrier((second, *state))
    shards = present + (second, swap_cores(second), third, swap_cores(third))

    def late(*refs):
        late_kernel(*refs, per=per, cpties=cpties)

    return pl.pallas_call(
        late,
        out_shape=[
            jax.ShapeDtypeStruct((cpties, paths), F32),
            jax.ShapeDtypeStruct((paths, width), BF16),
        ],
        in_specs=[vmem] * (len(state) + len(shards)),
        out_specs=[vmem, vmem],
        scratch_shapes=[
            pltpu.VMEM((trades, width), BF16),
            pltpu.VMEM((META_ROWS, trades), F32),
            pltpu.VMEM((1, groups), F32),
            pltpu.VMEM((paths, trades), BF16),
            pltpu.VMEM((trades, trades), BF16),
            pltpu.VMEM((trades, trades), BF16),
            pltpu.VMEM((paths, trades), F32),
            pltpu.VMEM((paths, trades), BF16),
        ],
        compiler_params=pltpu.CompilerParams(vmem_limit_bytes=36 << 20),
    )(*state, *shards)


def solution(mesh):
    placed = (
        P(("date", "path"), None),
        P(("date", "trade"), None),
        P("trade"),
        P("trade"),
        P(),
        P(),
        P("trade"),
    )
    small = mesh.shape["trade"] == 8 and mesh.shape["path"] == 2
    return jax.shard_map(
        gather_body if small else exchange_body,
        mesh=mesh,
        in_specs=placed,
        out_specs=(P("trade", ("date", "path")), P(("date", "path"), None)),
        check_vma=False,
    )
```

```python
import jax
import jax.numpy as jnp
from jax import lax
from jax.experimental import pallas as pl
from jax.experimental.pallas import tpu as pltpu
from jax.sharding import PartitionSpec as P

F32 = jnp.float32
BF16 = jnp.bfloat16
BLOCK = 256
META_ROWS = 8


def margin_terms(arrived, got_codes, risk_weights, correlation, funding_spread):
    path_rows = arrived.shape[0]
    cpty_count = funding_spread.shape[0]
    bucket_count = risk_weights.shape[0]
    is_filled = got_codes >= 0
    column_ids = jnp.arange(cpty_count * bucket_count, dtype=jnp.int32)
    hot_table = (got_codes[:, None] == column_ids[None, :]).astype(jnp.bfloat16)
    bucket_sums = jnp.dot(arrived, hot_table, preferred_element_type=jnp.float32)
    weighted = (
        bucket_sums.reshape(path_rows, cpty_count, bucket_count) * risk_weights[None, None, :]
    )
    rho_w = jnp.einsum("pcb,db->pcd", weighted, correlation, precision=lax.Precision.HIGHEST)
    margin_now = jnp.sqrt(jnp.sum(weighted * rho_w, axis=2) + 1e-06)
    sens_bar = (
        funding_spread[None, :, None] * risk_weights[None, None, :] * rho_w / margin_now[:, :, None]
    )
    flat_bar = sens_bar.reshape(path_rows, cpty_count * bucket_count)
    safe_codes = jnp.where(is_filled, got_codes, 0)
    slot_bar = jnp.take(flat_bar, safe_codes, axis=1) * is_filled[None, :].astype(jnp.float32)
    return (margin_now, slot_bar.astype(jnp.bfloat16))


def exchange_body(
    basis_values, coefficients, trade_cpty, trade_bucket, risk_weights, correlation, funding_spread
):
    owners = lax.axis_size("trade")
    per_device = coefficients.shape[0]
    capacity = max(2, 2 * per_device // owners)
    slot_total = owners * capacity
    cpty_count = funding_spread.shape[0]
    bucket_count = risk_weights.shape[0]
    path_rows = basis_values.shape[0]
    owner_of = trade_cpty // cpty_count
    trade_code = trade_cpty % cpty_count * bucket_count + trade_bucket
    position = jnp.arange(per_device, dtype=jnp.int32)
    same_owner = owner_of[:, None] == owner_of[None, :]
    earlier = position[None, :] < position[:, None]
    rank_in = jnp.sum((same_owner & earlier).astype(jnp.int32), axis=1)
    slot_index = owner_of * capacity + rank_in
    codes_out = jnp.full((slot_total,), -1, jnp.int32).at[slot_index].set(trade_code)
    got_codes = lax.all_to_all(codes_out, "trade", split_axis=0, concat_axis=0, tiled=True)
    delta_rows = lax.dot_general(
        basis_values, coefficients, (((1,), (1,)), ((), ())), preferred_element_type=jnp.float32
    ).astype(jnp.bfloat16)
    outgoing = jnp.zeros((path_rows, slot_total), jnp.bfloat16).at[:, slot_index].set(delta_rows)
    arrived = lax.all_to_all(outgoing, "trade", split_axis=1, concat_axis=1, tiled=True)
    margin_now, slot_bar = margin_terms(
        arrived, got_codes, risk_weights, correlation, funding_spread
    )
    returned = lax.all_to_all(slot_bar, "trade", split_axis=1, concat_axis=1, tiled=True)
    delta_bar = returned[:, slot_index]
    partial_adj = jnp.dot(delta_bar, coefficients, preferred_element_type=jnp.float32)
    basis_adjoint = lax.psum(partial_adj, "trade").astype(jnp.bfloat16)
    return (margin_now.T, basis_adjoint)


def dot(a, b):
    return jnp.dot(a, b, preferred_element_type=F32)


def split(x):
    hi = x.astype(BF16)
    return hi, (x - hi.astype(F32)).astype(BF16)


def one_hot_t(row, count):
    ids = lax.broadcasted_iota(jnp.int32, (count, row.shape[1]), 0).astype(F32)
    return (ids == row).astype(F32).astype(BF16)


def pack_kernel(*refs, cpties):
    sources, out_ref, scratch, sem = refs[:4], refs[4], refs[5:8], refs[8]
    per, width = sources[3].shape
    goals = (*scratch, out_ref.at[pl.ds(0, per)])
    copies = [pltpu.make_async_copy(s, g, sem.at[k]) for k, (s, g) in enumerate(zip(sources, goals))]
    for copy in copies:
        copy.start()
    for copy in copies[:3]:
        copy.wait()
    cpty, bucket, spread = (ref[...] for ref in scratch)
    owner = cpty // cpties
    high = spread.astype(BF16).astype(F32)
    middle = (spread - high).astype(BF16).astype(F32)
    rows = [owner, cpty - owner * cpties, bucket, high, middle, spread - high - middle]
    out_ref[per:] = jnp.zeros((META_ROWS, width), BF16)
    for k, row in enumerate(rows):
        out_ref[per + k : per + k + 1, : row.shape[1]] = row.astype(F32).astype(BF16)
    copies[3].wait()


def cut(start, stop):
    return [slice(k, min(k + BLOCK, stop)) for k in range(start, stop, BLOCK)]


def deltas(basis, coef, rows):
    return lax.dot_general(
        basis[...], coef[rows, :], (((1,), (1,)), ((), ())), preferred_element_type=F32
    ).astype(BF16)


def place_shards(coef, sides, both, core, per, start=0):
    spots = [s for s in range(len(both) + 1) if s != EITHER]
    for s, ref in zip(spots, both):
        if s >= start:
            coef[s * per : (s + 1) * per] = ref[:per]
    for side, ref in enumerate(sides):

        @pl.when(core == side)
        def _():
            coef[EITHER * per : (EITHER + 1) * per] = ref[:per]


def read_meta(tails, meta, spread, per, cpties):
    for s, tail in enumerate(tails):
        meta[:, s * per : (s + 1) * per] = tail[:, :per]
        spread[:, s * cpties : (s + 1) * cpties] = (
            tail[3:4, :cpties] + tail[4:5, :cpties] + tail[5:6, :cpties]
        )


def shard_tails(sides, both, core, per):
    tails = [ref[per : per + META_ROWS].astype(F32) for ref in both]
    zero, one = (ref[per : per + META_ROWS].astype(F32) for ref in sides)
    tails.insert(EITHER, jnp.where(core == 0, zero, one))
    return tails


def groups_of(meta, me, core, cpties):
    offset = meta[0:1, :].astype(jnp.int32) ^ me
    group = meta[1:2, :]
    for s in range(1, len(LAYOUT[0])):
        there = jnp.where(core == 0, LAYOUT[0][s], LAYOUT[1][s])
        group = group + jnp.where(offset == there, F32(s * cpties), F32(0))
    return group


def pair_factors(table, bucket_t):
    buckets = bucket_t.shape[0]
    bucket_hot = bucket_t.T
    right = [dot(table[k * buckets : (k + 1) * buckets], bucket_t).astype(BF16) for k in range(2)]
    return jnp.concatenate([bucket_hot, bucket_hot], 1), jnp.concatenate(right, 0)


def fill_pairs(left, right, group_col, group, m_hi, m_lo, rows, cols):
    pair = dot(left[rows], right[:, cols])
    pair = jnp.where(group_col[rows] == group[:, cols], pair, 0.0)
    m_hi[rows, cols], m_lo[rows, cols] = split(pair)


def column(row, lanes):
    return jnp.broadcast_to(row, (lanes, row.shape[1])).T[:, :1]


def advance(basis, coef, delta, m_hi, m_lo, factors, group_col, group, done, upto, prior, r_out):
    left, right = factors
    blocks = cut(0, upto)

    def fill(cols):
        for rows in blocks if cols.start >= done else cut(done, upto):
            fill_pairs(left, right, group_col, group, m_hi, m_lo, rows, cols)

    for cols in cut(done, upto):
        delta[:, cols] = deltas(basis, coef, cols)
    fill(blocks[0])
    for k, cols in enumerate(blocks):
        if k + 1 < len(blocks):
            fill(blocks[k + 1])
        inner = slice(0 if cols.start >= done else done, upto)
        r = dot(delta[:, inner], m_hi[inner, cols]) + dot(delta[:, inner], m_lo[inner, cols])
        r_out[:, cols] = r if cols.start >= done else prior[:, cols] + r


def early_kernel(basis_ref, weight_ref, corr_ref, *refs, per, cpties):
    sides, both = refs[:2], refs[2:5]
    delta, r_part, table, basis = refs[5:9]
    coef, weight, corr, meta, spread, m_hi, m_lo, sem = refs[9:]
    buckets = corr.shape[0]
    early = delta.shape[1]
    me, core = lax.axis_index("trade"), lax.axis_index("path")
    small = [
        pltpu.make_async_copy(weight_ref, weight, sem.at[0]),
        pltpu.make_async_copy(corr_ref, corr, sem.at[1]),
    ]
    whole = pltpu.make_async_copy(basis_ref, basis, sem.at[2])
    for copy in (*small, whole):
        copy.start()
    read_meta(shard_tails(sides, both, core, per), meta, spread, per, cpties)
    group = groups_of(meta[:, :early], me, core, cpties)
    bucket_t = one_hot_t(meta[2:3, :early], buckets)
    place_shards(coef, sides, both, core, per)
    for copy in small:
        copy.wait()
    weight_col = column(weight[...], buckets)
    hi, lo = split(corr[...] * weight[...] * weight_col)
    table[:buckets] = hi
    table[buckets:] = lo
    factors = pair_factors(table, bucket_t)
    whole.wait()
    advance(
        basis, coef, delta, m_hi, m_lo, factors, column(group, buckets), group, 0, early, None, r_part
    )


def middle_kernel(prior_delta, prior, table, basis, *refs, per, cpties):
    sides, both = refs[:2], refs[2:6]
    delta, r_part = refs[6:8]
    coef, meta, spread, m_hi, m_lo = refs[8:]
    done, upto = prior_delta.shape[1], delta.shape[1]
    buckets = table.shape[0] // 2
    me, core = lax.axis_index("trade"), lax.axis_index("path")
    read_meta(shard_tails(sides, both, core, per), meta, spread, per, cpties)
    group = groups_of(meta[:, :upto], me, core, cpties)
    factors = pair_factors(table, one_hot_t(meta[2:3, :upto], buckets))
    place_shards(coef, sides, both, core, per, EITHER)
    delta[:, :done] = prior_delta[...]
    advance(
        basis, coef, delta, m_hi, m_lo, factors, column(group, buckets), group, done, upto, prior, r_part
    )


def late_kernel(prior_delta, prior, table, basis, *refs, per, cpties):
    shards = len(LAYOUT[0])
    sides, both = refs[:2], refs[2 : shards + 1]
    margin_ref, adj_ref = refs[shards + 1 : shards + 3]
    coef, meta, spread, delta, m_hi, m_lo, r_all, bar = refs[shards + 3 :]
    done, trades = prior_delta.shape[1], coef.shape[0]
    groups = spread.shape[1]
    buckets = table.shape[0] // 2
    me, core = lax.axis_index("trade"), lax.axis_index("path")
    read_meta(shard_tails(sides, both, core, per), meta, spread, per, cpties)
    group = groups_of(meta, me, core, cpties)
    group_t = one_hot_t(group, groups)
    group_hot = group_t.T
    factors = pair_factors(table, one_hot_t(meta[2:3, :], buckets))
    place_shards(coef, sides, both, core, per)
    delta[:, :done] = prior_delta[...]
    advance(
        basis, coef, delta, m_hi, m_lo, factors, column(group, groups), group, done, trades, prior, r_all
    )
    blocks = cut(0, trades)
    squares = None
    for cols in blocks:
        hi, lo = split(delta[:, cols].astype(F32) * r_all[:, cols])
        part = dot(hi, group_hot[cols]) + dot(lo, group_hot[cols])
        squares = part if squares is None else squares + part
    margin = jnp.sqrt(squares + 1e-06)
    margin_ref[...] = margin.T[:cpties]
    hi, lo = split(spread[...] / margin)
    scale = jnp.concatenate([hi, lo], 1)
    group_two = jnp.concatenate([group_t, group_t], 0)
    for cols in blocks:
        bar[:, cols] = (r_all[:, cols] * dot(scale, group_two[:, cols])).astype(BF16)
    adj_ref[...] = dot(bar[...], coef[...]).astype(BF16)


def swap_cores(x):
    return lax.ppermute(x, "path", [(0, 1), (1, 0)])


def fetch(x, owners, *offsets):
    pairs = []
    for core, offset in enumerate(offsets):
        pairs += [((i ^ offset) * 2 + core, i * 2 + core) for i in range(owners)]
    return lax.ppermute(x, ("trade", "path"), pairs)


LAYOUT = ((0, 4, 2, 1, 5, 3, 6, 7), (0, 2, 4, 1, 3, 5, 7, 6))
EITHER = 3


def hold(x):
    return pltpu.with_memory_space_constraint(x, pltpu.HBM)


def gather_body(
    basis_values, coefficients, trade_cpty, trade_bucket, risk_weights, correlation, funding_spread
):
    owners = lax.axis_size("trade")
    per = coefficients.shape[0]
    cpties = funding_spread.shape[0]
    buckets = risk_weights.shape[0]
    paths, width = basis_values.shape
    trades = owners * per
    vmem = pl.BlockSpec(memory_space=pltpu.VMEM)
    anywhere = pl.BlockSpec(memory_space=pl.ANY)

    def pack(*refs):
        pack_kernel(*refs, cpties=cpties)

    payload = pl.pallas_call(
        pack,
        out_shape=jax.ShapeDtypeStruct((per + META_ROWS, width), BF16),
        in_specs=[anywhere] * 4,
        out_specs=vmem,
        scratch_shapes=[
            pltpu.VMEM((1, per), jnp.int32),
            pltpu.VMEM((1, per), jnp.int32),
            pltpu.VMEM((1, cpties), F32),
            pltpu.SemaphoreType.DMA((4,)),
        ],
        compiler_params=pltpu.CompilerParams(vmem_limit_bytes=4 << 20),
    )(
        hold(trade_cpty.reshape(1, per)),
        hold(trade_bucket.reshape(1, per)),
        hold(funding_spread.reshape(1, cpties)),
        hold(coefficients),
    )
    core = lax.axis_index("path")
    first = fetch(payload, owners, 4, 2)
    beside = fetch(payload, owners, 0, 1)
    first, beside = lax.optimization_barrier((first, beside))
    sent = jnp.where(core == 0, first, beside)
    second = fetch(sent, owners, 1, 2)
    first_other = swap_cores(first)
    _, first_other = lax.optimization_barrier((sent, first_other))
    opposite = jnp.where(core == 0, first, first_other)
    third = fetch(opposite, owners, 2, 3)
    present = (swap_cores(beside), beside, payload, first, first_other)
    early_trades = trades // 2 // BLOCK * BLOCK
    groups = owners * cpties

    def early(*refs):
        early_kernel(*refs, per=per, cpties=cpties)

    state = pl.pallas_call(
        early,
        out_shape=[
            jax.ShapeDtypeStruct((paths, early_trades), BF16),
            jax.ShapeDtypeStruct((paths, early_trades), F32),
            jax.ShapeDtypeStruct((2 * buckets, buckets), BF16),
            jax.ShapeDtypeStruct((paths, width), BF16),
        ],
        in_specs=[anywhere] * 3 + [vmem] * len(present),
        out_specs=[vmem] * 4,
        scratch_shapes=[
            pltpu.VMEM((trades // 2, width), BF16),
            pltpu.VMEM((1, buckets), F32),
            pltpu.VMEM((buckets, buckets), F32),
            pltpu.VMEM((META_ROWS, trades // 2), F32),
            pltpu.VMEM((1, groups // 2), F32),
            pltpu.VMEM((early_trades, early_trades), BF16),
            pltpu.VMEM((early_trades, early_trades), BF16),
            pltpu.SemaphoreType.DMA((3,)),
        ],
        cost_estimate=pl.CostEstimate(flops=2 * 10**9, bytes_accessed=4 * 10**6, transcendentals=0),
        compiler_params=pltpu.CompilerParams(vmem_limit_bytes=16 << 20),
    )(
        hold(basis_values),
        hold(risk_weights.reshape(1, buckets)),
        hold(correlation),
        *present,
    )
    second, *state = lax.optimization_barrier((second, *state))
    second_other = swap_cores(second)
    middle_trades = 5 * per // BLOCK * BLOCK

    def middle(*refs):
        middle_kernel(*refs, per=per, cpties=cpties)

    table, basis = state[2:]
    state = pl.pallas_call(
        middle,
        out_shape=[
            jax.ShapeDtypeStruct((paths, middle_trades), BF16),
            jax.ShapeDtypeStruct((paths, middle_trades), F32),
        ],
        in_specs=[vmem] * (len(state) + len(present) + 1),
        out_specs=[vmem] * 2,
        scratch_shapes=[
            pltpu.VMEM((5 * per, width), BF16),
            pltpu.VMEM((META_ROWS, 5 * per), F32),
            pltpu.VMEM((1, 5 * cpties), F32),
            pltpu.VMEM((middle_trades, middle_trades), BF16),
            pltpu.VMEM((middle_trades, middle_trades), BF16),
        ],
        cost_estimate=pl.CostEstimate(flops=1000, bytes_accessed=1000, transcendentals=0),
        compiler_params=pltpu.CompilerParams(vmem_limit_bytes=16 << 20),
    )(*state, *present, second)
    third, *state = lax.optimization_barrier((third, *state))
    state = (*state, table, basis)
    shards = present + (second, second_other, third, swap_cores(third))

    def late(*refs):
        late_kernel(*refs, per=per, cpties=cpties)

    return pl.pallas_call(
        late,
        out_shape=[
            jax.ShapeDtypeStruct((cpties, paths), F32),
            jax.ShapeDtypeStruct((paths, width), BF16),
        ],
        in_specs=[vmem] * (len(state) + len(shards)),
        out_specs=[vmem, vmem],
        scratch_shapes=[
            pltpu.VMEM((trades, width), BF16),
            pltpu.VMEM((META_ROWS, trades), F32),
            pltpu.VMEM((1, groups), F32),
            pltpu.VMEM((paths, trades), BF16),
            pltpu.VMEM((trades, trades), BF16),
            pltpu.VMEM((trades, trades), BF16),
            pltpu.VMEM((paths, trades), F32),
            pltpu.VMEM((paths, trades), BF16),
        ],
        compiler_params=pltpu.CompilerParams(vmem_limit_bytes=36 << 20),
    )(*state, *shards)


def solution(mesh):
    placed = (
        P(("date", "path"), None),
        P(("date", "trade"), None),
        P("trade"),
        P("trade"),
        P(),
        P(),
        P("trade"),
    )
    small = mesh.shape["trade"] == 8 and mesh.shape["path"] == 2
    return jax.shard_map(
        gather_body if small else exchange_body,
        mesh=mesh,
        in_specs=placed,
        out_specs=(P("trade", ("date", "path")), P(("date", "path"), None)),
        check_vma=False,
    )
```

```python
import jax
import jax.numpy as jnp
from jax import lax
from jax.experimental import pallas as pl
from jax.experimental.pallas import tpu as pltpu
from jax.sharding import PartitionSpec as P

F32 = jnp.float32
BF16 = jnp.bfloat16
BLOCK = 256
META_ROWS = 8


def margin_terms(arrived, got_codes, risk_weights, correlation, funding_spread):
    path_rows = arrived.shape[0]
    cpty_count = funding_spread.shape[0]
    bucket_count = risk_weights.shape[0]
    is_filled = got_codes >= 0
    column_ids = jnp.arange(cpty_count * bucket_count, dtype=jnp.int32)
    hot_table = (got_codes[:, None] == column_ids[None, :]).astype(jnp.bfloat16)
    bucket_sums = jnp.dot(arrived, hot_table, preferred_element_type=jnp.float32)
    weighted = (
        bucket_sums.reshape(path_rows, cpty_count, bucket_count) * risk_weights[None, None, :]
    )
    rho_w = jnp.einsum("pcb,db->pcd", weighted, correlation, precision=lax.Precision.HIGHEST)
    margin_now = jnp.sqrt(jnp.sum(weighted * rho_w, axis=2) + 1e-06)
    sens_bar = (
        funding_spread[None, :, None] * risk_weights[None, None, :] * rho_w / margin_now[:, :, None]
    )
    flat_bar = sens_bar.reshape(path_rows, cpty_count * bucket_count)
    safe_codes = jnp.where(is_filled, got_codes, 0)
    slot_bar = jnp.take(flat_bar, safe_codes, axis=1) * is_filled[None, :].astype(jnp.float32)
    return (margin_now, slot_bar.astype(jnp.bfloat16))


def exchange_body(
    basis_values, coefficients, trade_cpty, trade_bucket, risk_weights, correlation, funding_spread
):
    owners = lax.axis_size("trade")
    per_device = coefficients.shape[0]
    capacity = max(2, 2 * per_device // owners)
    slot_total = owners * capacity
    cpty_count = funding_spread.shape[0]
    bucket_count = risk_weights.shape[0]
    path_rows = basis_values.shape[0]
    owner_of = trade_cpty // cpty_count
    trade_code = trade_cpty % cpty_count * bucket_count + trade_bucket
    position = jnp.arange(per_device, dtype=jnp.int32)
    same_owner = owner_of[:, None] == owner_of[None, :]
    earlier = position[None, :] < position[:, None]
    rank_in = jnp.sum((same_owner & earlier).astype(jnp.int32), axis=1)
    slot_index = owner_of * capacity + rank_in
    codes_out = jnp.full((slot_total,), -1, jnp.int32).at[slot_index].set(trade_code)
    got_codes = lax.all_to_all(codes_out, "trade", split_axis=0, concat_axis=0, tiled=True)
    delta_rows = lax.dot_general(
        basis_values, coefficients, (((1,), (1,)), ((), ())), preferred_element_type=jnp.float32
    ).astype(jnp.bfloat16)
    outgoing = jnp.zeros((path_rows, slot_total), jnp.bfloat16).at[:, slot_index].set(delta_rows)
    arrived = lax.all_to_all(outgoing, "trade", split_axis=1, concat_axis=1, tiled=True)
    margin_now, slot_bar = margin_terms(
        arrived, got_codes, risk_weights, correlation, funding_spread
    )
    returned = lax.all_to_all(slot_bar, "trade", split_axis=1, concat_axis=1, tiled=True)
    delta_bar = returned[:, slot_index]
    partial_adj = jnp.dot(delta_bar, coefficients, preferred_element_type=jnp.float32)
    basis_adjoint = lax.psum(partial_adj, "trade").astype(jnp.bfloat16)
    return (margin_now.T, basis_adjoint)


def dot(a, b):
    return jnp.dot(a, b, preferred_element_type=F32)


def split(x):
    hi = x.astype(BF16)
    return hi, (x - hi.astype(F32)).astype(BF16)


def one_hot_t(row, count):
    ids = lax.broadcasted_iota(jnp.int32, (count, row.shape[1]), 0).astype(F32)
    return (ids == row).astype(F32).astype(BF16)


def pack_kernel(*refs, cpties):
    sources, out_ref, scratch, sem = refs[:4], refs[4], refs[5:8], refs[8]
    per, width = sources[3].shape
    goals = (*scratch, out_ref.at[pl.ds(0, per)])
    copies = [pltpu.make_async_copy(s, g, sem.at[k]) for k, (s, g) in enumerate(zip(sources, goals))]
    for copy in copies:
        copy.start()
    for copy in copies[:3]:
        copy.wait()
    cpty, bucket, spread = (ref[...] for ref in scratch)
    owner = cpty // cpties
    high = spread.astype(BF16).astype(F32)
    middle = (spread - high).astype(BF16).astype(F32)
    rows = [owner, cpty - owner * cpties, bucket, high, middle, spread - high - middle]
    out_ref[per:] = jnp.zeros((META_ROWS, width), BF16)
    for k, row in enumerate(rows):
        out_ref[per + k : per + k + 1, : row.shape[1]] = row.astype(F32).astype(BF16)
    copies[3].wait()


def cut(start, stop):
    return [slice(k, min(k + BLOCK, stop)) for k in range(start, stop, BLOCK)]


def deltas(basis, coef, rows):
    return lax.dot_general(
        basis[...], coef[rows, :], (((1,), (1,)), ((), ())), preferred_element_type=F32
    ).astype(BF16)


def place_shards(coef, sides, both, core, per, start=0):
    spots = [s for s in range(len(both) + 1) if s != EITHER]
    for s, ref in zip(spots, both):
        if s >= start:
            coef[s * per : (s + 1) * per] = ref[:per]
    for side, ref in enumerate(sides):

        @pl.when(core == side)
        def _():
            coef[EITHER * per : (EITHER + 1) * per] = ref[:per]


def read_meta(tails, meta, spread, per, cpties):
    for s, tail in enumerate(tails):
        meta[:, s * per : (s + 1) * per] = tail[:, :per]
        spread[:, s * cpties : (s + 1) * cpties] = (
            tail[3:4, :cpties] + tail[4:5, :cpties] + tail[5:6, :cpties]
        )


def shard_tails(sides, both, core, per):
    tails = [ref[per : per + META_ROWS].astype(F32) for ref in both]
    zero, one = (ref[per : per + META_ROWS].astype(F32) for ref in sides)
    tails.insert(EITHER, jnp.where(core == 0, zero, one))
    return tails


def groups_of(meta, me, core, cpties):
    offset = meta[0:1, :].astype(jnp.int32) ^ me
    group = meta[1:2, :]
    for s in range(1, len(LAYOUT[0])):
        there = jnp.where(core == 0, LAYOUT[0][s], LAYOUT[1][s])
        group = group + jnp.where(offset == there, F32(s * cpties), F32(0))
    return group


def pair_factors(table, bucket_t):
    buckets = bucket_t.shape[0]
    bucket_hot = bucket_t.T
    right = [dot(table[k * buckets : (k + 1) * buckets], bucket_t).astype(BF16) for k in range(2)]
    return jnp.concatenate([bucket_hot, bucket_hot], 1), jnp.concatenate(right, 0)


def fill_pairs(left, right, group_col, group, m_hi, m_lo, rows, cols):
    pair = dot(left[rows], right[:, cols])
    pair = jnp.where(group_col[rows] == group[:, cols], pair, 0.0)
    m_hi[rows, cols], m_lo[rows, cols] = split(pair)


def column(row, lanes):
    return jnp.broadcast_to(row, (lanes, row.shape[1])).T[:, :1]


def advance(basis, coef, delta, m_hi, m_lo, factors, group_col, group, done, upto, prior, r_out):
    left, right = factors
    blocks = cut(0, upto)

    def fill(cols):
        for rows in blocks if cols.start >= done else cut(done, upto):
            fill_pairs(left, right, group_col, group, m_hi, m_lo, rows, cols)

    for cols in cut(done, upto):
        delta[:, cols] = deltas(basis, coef, cols)
    fill(blocks[0])
    for k, cols in enumerate(blocks):
        if k + 1 < len(blocks):
            fill(blocks[k + 1])
        inner = slice(0 if cols.start >= done else done, upto)
        r = dot(delta[:, inner], m_hi[inner, cols]) + dot(delta[:, inner], m_lo[inner, cols])
        r_out[:, cols] = r if cols.start >= done else prior[:, cols] + r


def early_kernel(basis_ref, weight_ref, corr_ref, *refs, per, cpties):
    sides, both = refs[:2], refs[2:5]
    delta, r_part, table, basis = refs[5:9]
    coef, weight, corr, meta, spread, m_hi, m_lo, sem = refs[9:]
    buckets = corr.shape[0]
    early = delta.shape[1]
    me, core = lax.axis_index("trade"), lax.axis_index("path")
    small = [
        pltpu.make_async_copy(weight_ref, weight, sem.at[0]),
        pltpu.make_async_copy(corr_ref, corr, sem.at[1]),
    ]
    whole = pltpu.make_async_copy(basis_ref, basis, sem.at[2])
    for copy in (*small, whole):
        copy.start()
    read_meta(shard_tails(sides, both, core, per), meta, spread, per, cpties)
    group = groups_of(meta[:, :early], me, core, cpties)
    bucket_t = one_hot_t(meta[2:3, :early], buckets)
    place_shards(coef, sides, both, core, per)
    for copy in small:
        copy.wait()
    weight_col = column(weight[...], buckets)
    hi, lo = split(corr[...] * weight[...] * weight_col)
    table[:buckets] = hi
    table[buckets:] = lo
    factors = pair_factors(table, bucket_t)
    whole.wait()
    advance(
        basis, coef, delta, m_hi, m_lo, factors, column(group, buckets), group, 0, early, None, r_part
    )


def middle_kernel(prior_delta, prior, table, basis, *refs, per, cpties):
    sides, both = refs[:2], refs[2:6]
    delta, r_part = refs[6:8]
    coef, meta, spread, m_hi, m_lo = refs[8:]
    done, upto = prior_delta.shape[1], delta.shape[1]
    buckets = table.shape[0] // 2
    me, core = lax.axis_index("trade"), lax.axis_index("path")
    read_meta(shard_tails(sides, both, core, per), meta, spread, per, cpties)
    group = groups_of(meta[:, :upto], me, core, cpties)
    factors = pair_factors(table, one_hot_t(meta[2:3, :upto], buckets))
    place_shards(coef, sides, both, core, per, EITHER)
    delta[:, :done] = prior_delta[...]
    advance(
        basis, coef, delta, m_hi, m_lo, factors, column(group, buckets), group, done, upto, prior, r_part
    )


def late_kernel(prior_delta, prior, table, basis, *refs, per, cpties):
    shards = len(LAYOUT[0])
    sides, both = refs[:2], refs[2 : shards + 1]
    margin_ref, adj_ref = refs[shards + 1 : shards + 3]
    coef, meta, spread, delta, m_hi, m_lo, r_all, bar = refs[shards + 3 :]
    done, trades = prior_delta.shape[1], coef.shape[0]
    groups = spread.shape[1]
    buckets = table.shape[0] // 2
    me, core = lax.axis_index("trade"), lax.axis_index("path")
    read_meta(shard_tails(sides, both, core, per), meta, spread, per, cpties)
    group = groups_of(meta, me, core, cpties)
    group_t = one_hot_t(group, groups)
    group_hot = group_t.T
    factors = pair_factors(table, one_hot_t(meta[2:3, :], buckets))
    place_shards(coef, sides, both, core, per)
    delta[:, :done] = prior_delta[...]
    advance(
        basis, coef, delta, m_hi, m_lo, factors, column(group, groups), group, done, trades, prior, r_all
    )
    blocks = cut(0, trades)
    squares = None
    for cols in blocks:
        hi, lo = split(delta[:, cols].astype(F32) * r_all[:, cols])
        part = dot(hi, group_hot[cols]) + dot(lo, group_hot[cols])
        squares = part if squares is None else squares + part
    margin = jnp.sqrt(squares + 1e-06)
    margin_ref[...] = margin.T[:cpties]
    hi, lo = split(spread[...] / margin)
    scale = jnp.concatenate([hi, lo], 1)
    group_two = jnp.concatenate([group_t, group_t], 0)
    for cols in blocks:
        bar[:, cols] = (r_all[:, cols] * dot(scale, group_two[:, cols])).astype(BF16)
    adj_ref[...] = dot(bar[...], coef[...]).astype(BF16)


def swap_cores(x):
    return lax.ppermute(x, "path", [(0, 1), (1, 0)])


def fetch(x, owners, *offsets):
    pairs = []
    for core, offset in enumerate(offsets):
        pairs += [((i ^ offset) * 2 + core, i * 2 + core) for i in range(owners)]
    return lax.ppermute(x, ("trade", "path"), pairs)


LAYOUT = ((0, 4, 2, 1, 5, 3, 7, 6), (0, 2, 4, 1, 3, 5, 6, 7))
EITHER = 3


def hold(x):
    return pltpu.with_memory_space_constraint(x, pltpu.HBM)


def gather_body(
    basis_values, coefficients, trade_cpty, trade_bucket, risk_weights, correlation, funding_spread
):
    owners = lax.axis_size("trade")
    per = coefficients.shape[0]
    cpties = funding_spread.shape[0]
    buckets = risk_weights.shape[0]
    paths, width = basis_values.shape
    trades = owners * per
    vmem = pl.BlockSpec(memory_space=pltpu.VMEM)
    anywhere = pl.BlockSpec(memory_space=pl.ANY)

    def pack(*refs):
        pack_kernel(*refs, cpties=cpties)

    payload = pl.pallas_call(
        pack,
        out_shape=jax.ShapeDtypeStruct((per + META_ROWS, width), BF16),
        in_specs=[anywhere] * 4,
        out_specs=vmem,
        scratch_shapes=[
            pltpu.VMEM((1, per), jnp.int32),
            pltpu.VMEM((1, per), jnp.int32),
            pltpu.VMEM((1, cpties), F32),
            pltpu.SemaphoreType.DMA((4,)),
        ],
        compiler_params=pltpu.CompilerParams(vmem_limit_bytes=4 << 20),
    )(
        hold(trade_cpty.reshape(1, per)),
        hold(trade_bucket.reshape(1, per)),
        hold(funding_spread.reshape(1, cpties)),
        hold(coefficients),
    )
    core = lax.axis_index("path")
    first = fetch(payload, owners, 4, 2)
    beside = fetch(payload, owners, 0, 1)
    first, beside = lax.optimization_barrier((first, beside))
    sent = jnp.where(core == 0, first, beside)
    second = fetch(sent, owners, 1, 2)
    first_other = swap_cores(first)
    _, first_other = lax.optimization_barrier((sent, first_other))
    opposite = jnp.where(core == 0, first, first_other)
    third = fetch(opposite, owners, 3, 2)
    present = (swap_cores(beside), beside, payload, first, first_other)
    early_trades = trades // 2 // BLOCK * BLOCK
    groups = owners * cpties

    def early(*refs):
        early_kernel(*refs, per=per, cpties=cpties)

    state = pl.pallas_call(
        early,
        out_shape=[
            jax.ShapeDtypeStruct((paths, early_trades), BF16),
            jax.ShapeDtypeStruct((paths, early_trades), F32),
            jax.ShapeDtypeStruct((2 * buckets, buckets), BF16),
            jax.ShapeDtypeStruct((paths, width), BF16),
        ],
        in_specs=[anywhere] * 3 + [vmem] * len(present),
        out_specs=[vmem] * 4,
        scratch_shapes=[
            pltpu.VMEM((trades // 2, width), BF16),
            pltpu.VMEM((1, buckets), F32),
            pltpu.VMEM((buckets, buckets), F32),
            pltpu.VMEM((META_ROWS, trades // 2), F32),
            pltpu.VMEM((1, groups // 2), F32),
            pltpu.VMEM((early_trades, early_trades), BF16),
            pltpu.VMEM((early_trades, early_trades), BF16),
            pltpu.SemaphoreType.DMA((3,)),
        ],
        cost_estimate=pl.CostEstimate(flops=2 * 10**9, bytes_accessed=4 * 10**6, transcendentals=0),
        compiler_params=pltpu.CompilerParams(vmem_limit_bytes=16 << 20),
    )(
        hold(basis_values),
        hold(risk_weights.reshape(1, buckets)),
        hold(correlation),
        *present,
    )
    second, *state = lax.optimization_barrier((second, *state))
    second_other = swap_cores(second)
    middle_trades = 5 * per // BLOCK * BLOCK

    def middle(*refs):
        middle_kernel(*refs, per=per, cpties=cpties)

    table, basis = state[2:]
    state = pl.pallas_call(
        middle,
        out_shape=[
            jax.ShapeDtypeStruct((paths, middle_trades), BF16),
            jax.ShapeDtypeStruct((paths, middle_trades), F32),
        ],
        in_specs=[vmem] * (len(state) + len(present) + 1),
        out_specs=[vmem] * 2,
        scratch_shapes=[
            pltpu.VMEM((5 * per, width), BF16),
            pltpu.VMEM((META_ROWS, 5 * per), F32),
            pltpu.VMEM((1, 5 * cpties), F32),
            pltpu.VMEM((middle_trades, middle_trades), BF16),
            pltpu.VMEM((middle_trades, middle_trades), BF16),
        ],
        cost_estimate=pl.CostEstimate(flops=1000, bytes_accessed=1000, transcendentals=0),
        compiler_params=pltpu.CompilerParams(vmem_limit_bytes=16 << 20),
    )(*state, *present, second)
    third, *state = lax.optimization_barrier((third, *state))
    state = (*state, table, basis)
    shards = present + (second, second_other, third, swap_cores(third))

    def late(*refs):
        late_kernel(*refs, per=per, cpties=cpties)

    return pl.pallas_call(
        late,
        out_shape=[
            jax.ShapeDtypeStruct((cpties, paths), F32),
            jax.ShapeDtypeStruct((paths, width), BF16),
        ],
        in_specs=[vmem] * (len(state) + len(shards)),
        out_specs=[vmem, vmem],
        scratch_shapes=[
            pltpu.VMEM((trades, width), BF16),
            pltpu.VMEM((META_ROWS, trades), F32),
            pltpu.VMEM((1, groups), F32),
            pltpu.VMEM((paths, trades), BF16),
            pltpu.VMEM((trades, trades), BF16),
            pltpu.VMEM((trades, trades), BF16),
            pltpu.VMEM((paths, trades), F32),
            pltpu.VMEM((paths, trades), BF16),
        ],
        compiler_params=pltpu.CompilerParams(vmem_limit_bytes=36 << 20),
    )(*state, *shards)


def solution(mesh):
    placed = (
        P(("date", "path"), None),
        P(("date", "trade"), None),
        P("trade"),
        P("trade"),
        P(),
        P(),
        P("trade"),
    )
    small = mesh.shape["trade"] == 8 and mesh.shape["path"] == 2
    return jax.shard_map(
        gather_body if small else exchange_body,
        mesh=mesh,
        in_specs=placed,
        out_specs=(P("trade", ("date", "path")), P(("date", "path"), None)),
        check_vma=False,
    )
```
